32 devices in a mesh: rep: 8 (over y, x, core), tp: 4 (over z).
Axes of the slice: x: 2, y: 2, z: 4, core: 2. Of those that a mesh axis runs over, the one named last changes fastest.
Arguments:
- tokens: bfloat16 [4096, 8192], P('rep', 'tp'), may hold values from -6 to 6
- query_weight: bfloat16 [8192, 4096], P(None, 'tp'), may hold values from -0.0625 to 0.0625
- key_value_weight: bfloat16 [8192, 1024], P('tp'), may hold values from -0.0625 to 0.0625
- adapter_down_tables: bfloat16 [32, 192, 8192], P('rep', None, 'tp'), may hold values from -0.0625 to 0.0625
- adapter_up_query: bfloat16 [32, 64, 4096], P('rep', None, 'tp'), may hold values from -0.75 to 0.75
- adapter_up_key_value: bfloat16 [32, 64, 1024], P('rep', None, 'tp'), may hold values from -0.75 to 0.75
- request_adapter: int32 [128], P('rep'), may hold values from 0 to 31, as said below
- request_token_length: int32 [128], P('rep'), may hold values from 8 to 32, as said below
- adapter_table_row: int32 [32], replicated, may hold values from 0 to 31, as said below
Outputs:
- attended: bfloat16 [4096, 4096], P('rep', 'tp')
The draws below stay inside these ranges and needn't reach their ends.
Inputs may be any that keep to these rules, and one draw needn't show every extreme that they name: `request_adapter`: in each replica's block of 16 requests at most 4 have adapters whose table rows adapter_table_row lies in one index of rep's share (rows s with the same s // 4); in every draw one share gets exactly 4 from every replica. `adapter_table_row`: A permutation of the table rows. `request_token_length`: every replica has one request of exactly 32 tokens.
All inputs are finite; a program needn't handle non-finite values.
Results may differ from the reference program's by a relative error of at most 0.0098.
Values may be sent and summed in bfloat16 or wider, within the bound.
A program may use at most 192 MiB of HBM per device.

```python
import math
import jax
import jax.numpy as jnp
from jax import lax

MODEL_WIDTH = 8192
HEAD_SIZE = 128
QUERY_HEADS = 32
KEY_VALUE_HEADS = 4
ADAPTER_RANK = 64
ADAPT_DEV = 4
REQS_DEV = 16
SEQ = 32
REQUESTS = 128
TOKENS = 4096
ADAPTER_COUNT = 32
CAP_REQ = 4


def draw_tokens(key, part):
    return jnp.clip(jax.random.normal(key, (TOKENS, MODEL_WIDTH), jnp.float32), -6.0, 6.0).astype(jnp.bfloat16)


def table_homes(key):
    return jax.random.permutation(jax.random.fold_in(key, 11), ADAPTER_COUNT).astype(jnp.int32)


def draw_adapter_table_row(key, part):
    return table_homes(key)


def draw_request_adapter(key, part):
    homes = table_homes(key)
    holder = jnp.zeros((ADAPTER_COUNT,), jnp.int32).at[homes].set(jnp.arange(ADAPTER_COUNT, dtype=jnp.int32))
    replicas = REQUESTS // REQS_DEV
    slot_total = replicas * CAP_REQ
    base_key = jax.random.fold_in(key, 23)
    busiest = jax.random.randint(jax.random.fold_in(base_key, 1), (), 0, replicas, dtype=jnp.int32)
    slot_owner = jnp.arange(slot_total, dtype=jnp.int32) // CAP_REQ

    def one_replica(replica_index):
        replica_key = jax.random.fold_in(base_key, replica_index + 2)
        order_key, shuffle_key, local_key = jax.random.split(replica_key, 3)
        ranking = jax.random.permutation(order_key, slot_total).astype(jnp.int32)
        priority = jnp.where(slot_owner == busiest, ranking - slot_total, ranking)
        chosen = jnp.argsort(priority, stable=True)[:REQS_DEV].astype(jnp.int32)
        owners = slot_owner[chosen]
        shuffle_order = jax.random.permutation(shuffle_key, REQS_DEV).astype(jnp.int32)
        owners = owners[shuffle_order]
        local_pick = jax.random.randint(local_key, (REQS_DEV,), 0, ADAPT_DEV, dtype=jnp.int32)
        return holder[owners * ADAPT_DEV + local_pick]
    picked = jax.vmap(one_replica)(jnp.arange(replicas, dtype=jnp.int32))
    return picked.reshape(REQUESTS).astype(jnp.int32)


def draw_request_token_length(key, part):
    replicas = REQUESTS // REQS_DEV
    first_key, second_key = jax.random.split(key)
    drawn = jax.random.randint(first_key, (replicas, REQS_DEV), max(1, SEQ // 4), SEQ + 1, dtype=jnp.int32)
    longest = jax.random.randint(second_key, (replicas, 1), 0, REQS_DEV, dtype=jnp.int32)
    filled = jnp.where(jnp.arange(REQS_DEV, dtype=jnp.int32)[None, :] == longest, SEQ, drawn)
    return filled.reshape(REQUESTS).astype(jnp.int32)


def levels(rng, dims, cuts, low, top_value):
    def one(axis_at, parts):
        heights = jax.random.uniform(jax.random.fold_in(jax.random.fold_in(rng, 6), axis_at), (parts,), jnp.float32, low / len(cuts), top_value / len(cuts))
        return jnp.repeat(jnp.exp(heights), dims[axis_at] // parts).reshape((-1,) + (1,) * (len(dims) - axis_at - 1))

    level = one(*cuts[0])
    for cut in cuts[1:]:
        level = level * one(*cut)
    return level


def noise(own_key, shape, width, reach, pieces=(), held_as=jnp.bfloat16):
    loudness = levels(own_key, shape, pieces, -0.22, 0.18) if pieces else 1.0
    values = jax.random.normal(own_key, shape, jnp.float32) * width * loudness
    return jnp.minimum(jnp.maximum(values, -reach), reach).astype(held_as)


def setup_inputs(seed: int = 0) -> dict:
    seeds = jax.random.split(jax.random.key(seed), 10)
    tokens = draw_tokens(jax.random.fold_in(seeds[9], 71), 0)
    query_weight = noise(seeds[1], (MODEL_WIDTH, QUERY_HEADS * HEAD_SIZE), MODEL_WIDTH ** -0.5, 0.0625, ((1, 4),))
    key_value_weight = noise(seeds[2], (MODEL_WIDTH, 2 * KEY_VALUE_HEADS * HEAD_SIZE), MODEL_WIDTH ** -0.5, 0.0625, ((0, 4),))
    adapter_down_tables = noise(seeds[3], (ADAPTER_COUNT, 3 * ADAPTER_RANK, MODEL_WIDTH), MODEL_WIDTH ** -0.5, 0.0625, ((0, 8), (2, 4)))
    adapter_up_query = noise(seeds[4], (ADAPTER_COUNT, ADAPTER_RANK, QUERY_HEADS * HEAD_SIZE), ADAPTER_RANK ** -0.5, 0.75, ((0, 8), (2, 4)))
    adapter_up_key_value = noise(seeds[5], (ADAPTER_COUNT, ADAPTER_RANK, 2 * KEY_VALUE_HEADS * HEAD_SIZE), ADAPTER_RANK ** -0.5, 0.75, ((0, 8), (2, 4)))
    request_adapter = draw_request_adapter(jax.random.fold_in(seeds[9], 71), 0)
    request_token_length = draw_request_token_length(jax.random.fold_in(seeds[9], 71), 0)
    adapter_table_row = draw_adapter_table_row(jax.random.fold_in(seeds[9], 71), 0)
    return {"tokens": tokens, "query_weight": query_weight, "key_value_weight": key_value_weight, "adapter_down_tables": adapter_down_tables, "adapter_up_query": adapter_up_query, "adapter_up_key_value": adapter_up_key_value, "request_adapter": request_adapter, "request_token_length": request_token_length, "adapter_table_row": adapter_table_row}


adapter_scale = 0.5
rope_theta = 500000.0

def rotary(values, positions):
    half_dim = values.shape[-1] // 2
    frequency = rope_theta ** (-(jnp.arange(half_dim, dtype=jnp.float32) * 2.0 / values.shape[-1]))
    angles = positions.astype(jnp.float32)[:, None] * frequency[None, :]
    cosine = jnp.cos(angles)[:, None, :]
    sine_part = jnp.sin(angles)[:, None, :]
    lower_half = values[..., :half_dim]
    upper_half = values[..., half_dim:]
    return jnp.concatenate([lower_half * cosine - upper_half * sine_part, upper_half * cosine + lower_half * sine_part], axis=-1)

def reference(tokens, query_weight, key_value_weight, adapter_down_tables, adapter_up_query, adapter_up_key_value, request_adapter, request_token_length, adapter_table_row):
    base_query = jnp.dot(tokens, query_weight, preferred_element_type=jnp.float32)
    base_pair = jnp.dot(tokens, key_value_weight, preferred_element_type=jnp.float32)
    table_rows = adapter_table_row[request_adapter].astype(jnp.int32)
    key_columns = jnp.arange(2 * KEY_VALUE_HEADS * HEAD_SIZE, dtype=jnp.int32) < KEY_VALUE_HEADS * HEAD_SIZE
    request_rows = tokens.reshape(REQUESTS, SEQ, MODEL_WIDTH)

    def one_request(inputs):
        rows_x, adapter_row_index = inputs
        down_projection_rows = lax.dynamic_index_in_dim(adapter_down_tables, adapter_row_index, 0, keepdims=False)
        query_up_weight = lax.dynamic_index_in_dim(adapter_up_query, adapter_row_index, 0, keepdims=False)
        key_value_up_weight = lax.dynamic_index_in_dim(adapter_up_key_value, adapter_row_index, 0, keepdims=False)
        shrink = lax.dot_general(rows_x, down_projection_rows, (((1,), (1,)), ((), ())), preferred_element_type=jnp.float32).astype(jnp.bfloat16)
        query_update = jnp.dot(shrink[:, :ADAPTER_RANK], query_up_weight, preferred_element_type=jnp.float32)
        key_part = jnp.dot(shrink[:, ADAPTER_RANK:2 * ADAPTER_RANK], key_value_up_weight, preferred_element_type=jnp.float32)
        value_part = jnp.dot(shrink[:, 2 * ADAPTER_RANK:], key_value_up_weight, preferred_element_type=jnp.float32)
        key_value_delta = jnp.where(key_columns[None, :], key_part, value_part)
        return (adapter_scale * jnp.concatenate([query_update, key_value_delta], axis=1)).astype(jnp.bfloat16)
    delta = lax.map(one_request, (request_rows, table_rows))
    delta = delta.reshape(TOKENS, QUERY_HEADS * HEAD_SIZE + 2 * KEY_VALUE_HEADS * HEAD_SIZE).astype(jnp.float32)
    positions = jnp.arange(TOKENS, dtype=jnp.int32) % SEQ
    query = rotary((base_query + delta[:, :QUERY_HEADS * HEAD_SIZE]).reshape(TOKENS, QUERY_HEADS, HEAD_SIZE), positions).astype(jnp.bfloat16)
    pair_raw = (base_pair + delta[:, QUERY_HEADS * HEAD_SIZE:]).astype(jnp.bfloat16)
    pair_raw = lax.optimization_barrier(pair_raw)
    keys_raw = pair_raw[:, :KEY_VALUE_HEADS * HEAD_SIZE].reshape(TOKENS, KEY_VALUE_HEADS, HEAD_SIZE)
    values = pair_raw[:, KEY_VALUE_HEADS * HEAD_SIZE:].reshape(REQUESTS, SEQ, KEY_VALUE_HEADS, HEAD_SIZE)
    keys = rotary(keys_raw.astype(jnp.float32), positions).astype(jnp.bfloat16)
    group_size = QUERY_HEADS // KEY_VALUE_HEADS
    query_full = query.astype(jnp.float32).reshape(REQUESTS, SEQ, KEY_VALUE_HEADS, group_size, HEAD_SIZE)
    keys_full = keys.astype(jnp.float32).reshape(REQUESTS, SEQ, KEY_VALUE_HEADS, HEAD_SIZE)
    scores = jnp.einsum('rqkgd,rpkd->rkgqp', query_full, keys_full) / math.sqrt(HEAD_SIZE)
    slot_pos = jnp.arange(SEQ, dtype=jnp.int32)
    allowed = (slot_pos[None, None, :] <= slot_pos[None, :, None]) & (slot_pos[None, None, :] < request_token_length[:, None, None])
    scores = jnp.where(allowed[:, None, None, :, :], scores, jnp.float32(-1e+30))
    peak = lax.optimization_barrier(jnp.max(scores, axis=-1, keepdims=True))
    weights = jnp.exp(scores - peak)
    probs = (weights / lax.optimization_barrier(jnp.sum(weights, axis=-1, keepdims=True))).astype(jnp.bfloat16)
    mixed = jnp.einsum('rkgqp,rpkd->rqkgd', probs.astype(jnp.float32), values.astype(jnp.float32))
    live = slot_pos[None, :] < request_token_length[:, None]
    mixed = jnp.where(live[:, :, None, None, None], mixed, jnp.float32(0.0))
    return mixed.astype(jnp.bfloat16).reshape(TOKENS, QUERY_HEADS * HEAD_SIZE)
```

```python
import math

import jax
import jax.numpy as jnp
import numpy as np
from jax import lax
from jax.experimental import pallas as pl
from jax.experimental.pallas import tpu as pltpu
from jax.sharding import PartitionSpec as P

HEAD_SIZE = 128
HALF = HEAD_SIZE // 2
SIDES = 3
LOW = 256
CHUNKS = 8
LEAD = 2

adapter_scale = 0.5
rope_theta = 500000.0
MESH = pl.DeviceIdType.MESH


def rope_tables(seq_len):
    frequency = np.float64(rope_theta) ** (-(np.arange(HALF, dtype=np.float64) * 2.0 / HEAD_SIZE))
    angles = np.arange(seq_len).astype(np.float64)[:, None] * frequency[None, :]
    cosine = np.concatenate([np.cos(angles), np.cos(angles)], axis=1)
    sine = np.concatenate([-np.sin(angles), np.sin(angles)], axis=1)
    return cosine.astype(np.float32), sine.astype(np.float32)


def nt_dot(a, b):
    return lax.dot_general(a, b, (((1,), (1,)), ((), ())), preferred_element_type=jnp.float32)


class Sizes:
    def __init__(self, replicas, tps, tokens, wq, wkv, tables, rank, requests, portion):
        self.reps = replicas
        self.tps = tps
        self.rows, self.feat = tokens
        self.qcols = wq[1]
        self.pcols = wkv[1]
        self.tables = tables
        self.rank = rank
        self.outs = SIDES * rank
        self.requests = requests
        self.seq = self.rows // requests
        self.cap = max(1, 2 * requests // replicas)
        self.slots = self.cap * replicas
        self.kv_heads = self.pcols // (2 * HEAD_SIZE)
        self.sharing = tps // self.kv_heads
        self.portion = portion
        self.chunk = self.rows // CHUNKS
        self.piece = self.rows // tps
        self.hooks = CHUNKS * (tps - 1)


def fused_kernel(z, *refs):
    names = (
        "meta", "marks", "cosine", "sine", "tokens", "by_request", "wq", "wkv", "down", "upq",
        "upkv", "out", "T", "G", "W", "WKV", "DN", "S", "RX", "MR", "SR", "RB", "PH", "RSB", "SH",
        "UQ", "UKV", "ACC", "PO", "CR", "CL", "OB", "loc", "outs", "gs", "gr", "as_", "ar", "ms",
        "mr", "ts", "tr", "cs", "cr", "rss", "rsr", "ags", "agr", "uks", "ukr", "uqs", "uqr",
        "uqf", "ves", "ver", "vef",
    )
    v = dict(zip(names, refs))
    meta, marks, tokens, out = v["meta"], v["marks"], v["tokens"], v["out"]
    G, W, WKV, DN, S, RX, MR, SR, RB = (v[n] for n in names[names.index("G") : names.index("PH")])
    PH, RSB, SH, UQ, UKV, ACC, PO, CR, CL, OB = (
        v[n] for n in names[names.index("PH") : names.index("loc")]
    )
    loc = v["loc"]
    rep = lax.axis_index("rep")
    tp = lax.axis_index("tp")
    last = z.tps - 1
    head = tp // z.sharing
    at_slots, at_ids, at_homes, at_sizes = 0, z.slots, z.slots + z.requests, z.slots + 2 * z.requests

    def remote(src, dst, send, recv, to):
        return pltpu.make_async_remote_copy(
            src_ref=src, dst_ref=dst, send_sem=send, recv_sem=recv, device_id=to, device_id_type=MESH
        )

    def other_tp(d):
        return lax.rem(tp + d, z.tps)

    T = v["T"]
    load_tokens = pltpu.make_async_copy(tokens, G.at[tp], loc.at[0])
    load_requests = pltpu.make_async_copy(v["by_request"], T, loc.at[5])
    load_wkv = pltpu.make_async_copy(v["wkv"], WKV, loc.at[1])
    load_w = pltpu.make_async_copy(v["wq"], W, loc.at[2])
    load_down = pltpu.make_async_copy(v["down"], DN, loc.at[3])
    my_tables = pl.ds(rep * z.tables, z.tables)
    load_upq = pltpu.make_async_copy(v["upq"], UQ.at[my_tables], loc.at[4])
    for c in (load_tokens, load_requests, load_wkv, load_w, load_down, load_upq):
        c.start()

    barrier = pltpu.get_barrier_semaphore()
    for k in range(1, z.reps):
        pl.semaphore_signal(barrier, inc=1, device_id=(jnp.bitwise_xor(rep, k), tp), device_id_type=MESH)
    for d in range(1, z.tps):
        pl.semaphore_signal(barrier, inc=1, device_id=(rep, other_tp(d)), device_id_type=MESH)
    pl.semaphore_wait(barrier, z.reps - 1 + z.tps - 1)

    def chunk_rows(i):
        return pl.ds(pl.multiple_of(i * z.chunk, z.chunk), z.chunk)

    def hop(side, s, i):
        to = lax.rem(tp + 1, z.tps) if side == 0 else lax.rem(tp + last, z.tps)
        part = G.at[s, chunk_rows(i)]
        return remote(part, part, v["gs"].at[side, s, i], v["gr"].at[side, s, i], (rep, to))

    def send_own(i):
        @pl.when(tp < last)
        def _():
            hop(0, tp, i).start()

        @pl.when(tp > 0)
        def _():
            hop(1, tp, i).start()

    def table_side(side, c):
        column = (c // z.sharing) * HEAD_SIZE + side * z.kv_heads * HEAD_SIZE
        return column // z.portion, column % z.portion

    def table_dst(side):
        return UKV.at[my_tables, :, pl.ds(side * HEAD_SIZE, HEAD_SIZE)]

    for c in range(z.tps):
        for side in range(2):
            owner, column = table_side(side, c)
            src = v["upkv"].at[:, :, pl.ds(column, HEAD_SIZE)]
            if owner == c:

                @pl.when(tp == c)
                def _():
                    pltpu.make_async_copy(src, table_dst(side), v["ukr"].at[side]).start()

            else:

                @pl.when(tp == owner)
                def _():
                    remote(src, table_dst(side), v["uks"].at[side, c], v["ukr"].at[side], (rep, c)).start()

    load_tokens.wait()
    for i in range(LEAD):
        send_own(i)

    def group(q):
        return pl.ds(q * z.cap, z.cap)

    def pack(q, dst):
        for j in range(z.cap):
            pick = meta[at_slots + q * z.cap + j]
            dst[q, j * z.seq : (j + 1) * z.seq, :] = T[pick]

    def token_copy(q):
        return remote(S.at[q], RX.at[rep], v["as_"].at[q], v["ar"].at[rep], (q, tp))

    def mark_copy(q):
        return remote(marks.at[q], MR.at[rep], v["ms"].at[q], v["mr"].at[rep], (q, tp))

    def return_copy(q):
        return remote(SR.at[group(q)], RB.at[group(rep)], v["ts"].at[q], v["tr"].at[rep], (q, tp))

    load_requests.wait()

    @pl.loop(1, z.reps)
    def _(k):
        q = jnp.bitwise_xor(rep, k)
        pack(q, S)
        token_copy(q).start()
        mark_copy(q).start()

    pack(rep, RX)
    MR[rep] = marks[rep]

    def pair_sums():
        load_wkv.wait()
        half = z.kv_heads * HEAD_SIZE

        @pl.loop(0, z.rows // 128)
        def _(b):
            rows = pl.ds(pl.multiple_of(b * 128, 128), 128)
            x = G[tp, rows, :]
            for side in range(2):
                r = jnp.dot(x, WKV[:, side * half : (side + 1) * half], preferred_element_type=jnp.float32)
                for h in range(z.kv_heads):
                    PO[h, rows, side * HEAD_SIZE : (side + 1) * HEAD_SIZE] = r[
                        :, h * HEAD_SIZE : (h + 1) * HEAD_SIZE
                    ]

    def pair_hop(side, c):
        to = lax.rem(tp + 1, z.tps) if side == 0 else lax.rem(tp + last, z.tps)
        buf = (CR if side == 0 else CL).at[c]
        return remote(buf, buf, v["cs"].at[side, c], v["cr"].at[side, c], (rep, to))

    def pair_step(n):
        for c in reversed(range(z.tps)):
            if c > n:

                @pl.when(tp == n)
                def _():
                    own = PO[c // z.sharing]
                    if n > 0:
                        pair_hop(0, c).wait_recv()
                        own = own + CR[c].astype(jnp.float32)
                    CR[c] = own.astype(jnp.bfloat16)
                    pair_hop(0, c).start()

        for c in range(z.tps):
            if c < last - n:

                @pl.when(tp == last - n)
                def _():
                    own = PO[c // z.sharing]
                    if n > 0:
                        pair_hop(1, c).wait_recv()
                        own = own + CL[c].astype(jnp.float32)
                    CL[c] = own.astype(jnp.bfloat16)
                    pair_hop(1, c).start()

    def pair_finish():
        @pl.when(tp > 0)
        def _():
            pair_hop(0, tp).wait_recv()
            PO[head] = PO[head] + CR[tp].astype(jnp.float32)

        @pl.when(tp < last)
        def _():
            pair_hop(1, tp).wait_recv()
            PO[head] = PO[head] + CL[tp].astype(jnp.float32)

    def shrink_of(q):
        x = RX[q]
        parts = [nt_dot(x, DN[a * z.outs : (a + 1) * z.outs, :]) for a in range(z.tables)]
        for j in range(z.cap):
            mark = MR[q, j : j + 1, 0:1]
            total = jnp.zeros((z.seq, z.outs), jnp.float32)
            for a in range(z.tables):
                total = jnp.where(mark == float(a), parts[a][j * z.seq : (j + 1) * z.seq], total)
            low = jnp.concatenate([total, jnp.zeros((z.seq, LOW - z.outs), jnp.float32)], axis=1)
            SR[q * z.cap + j] = low.astype(jnp.bfloat16)

    def up_copies(q, source, send_q, send_v):
        part = pl.ds(source * z.tables, z.tables)
        return (
            remote(UQ.at[part], UQ.at[part], send_q, v["uqr"].at[source], (q, tp)),
            remote(UKV.at[part], UKV.at[part], send_v, v["ver"].at[source], (q, tp)),
        )

    def peer_copies(k):
        q = jnp.bitwise_xor(rep, k)
        return up_copies(q, rep, v["uqs"].at[k], v["ves"].at[k])

    def sibling_copies(k):
        return up_copies(jnp.bitwise_xor(rep, 1), jnp.bitwise_xor(rep, k), v["uqf"].at[k], v["vef"].at[k])

    def shrink_step():
        load_down.wait()

        @pl.loop(0, z.reps)
        def _(k):
            q = jnp.bitwise_xor(rep, k)

            @pl.when(k > 0)
            def _():
                token_copy(q).wait_send()
                mark_copy(q).wait_send()
                remote(S.at[q], RX.at[q], v["as_"].at[q], v["ar"].at[q], (q, tp)).wait_recv()
                remote(marks.at[q], MR.at[q], v["ms"].at[q], v["mr"].at[q], (q, tp)).wait_recv()

            shrink_of(q)

            @pl.when(k > 0)
            def _():
                return_copy(q).start()

        RB[group(rep)] = SR[group(rep)]
        load_upq.wait()
        for side in range(2):
            pltpu.make_async_copy(table_dst(side), table_dst(side), v["ukr"].at[side]).wait()
        for k in range(2, z.reps, 2):
            for c in peer_copies(k):
                c.start()
        for c in sibling_copies(0):
            c.start()

    def up_forward():
        for k in range(2, z.reps, 2):
            q = jnp.bitwise_xor(rep, k)
            for c in up_copies(q, q, v["uqs"].at[k], v["ves"].at[k]):
                c.wait_recv()
            for c in sibling_copies(k):
                c.start()

    def up_finish():
        for k in range(0, z.reps, 2):
            q = jnp.bitwise_xor(rep, k + 1)
            for c in up_copies(q, q, v["uqf"].at[k], v["vef"].at[k]):
                c.wait_recv()

    def piece(c):
        return pl.ds(pl.multiple_of(c * z.piece, z.piece), z.piece)

    def scatter_copy(c):
        return remote(PH.at[piece(c)], RSB.at[tp], v["rss"].at[c], v["rsr"].at[tp], (rep, c))

    def gather_copy(c):
        return remote(SH.at[piece(tp)], SH.at[piece(tp)], v["ags"].at[c], v["agr"].at[tp], (rep, c))

    def home_step():
        @pl.loop(1, z.reps)
        def _(k):
            q = jnp.bitwise_xor(rep, k)
            remote(SR.at[group(q)], RB.at[group(q)], v["ts"].at[q], v["tr"].at[q], (q, tp)).wait_recv()

        @pl.loop(0, z.requests)
        def _(r):
            PH[pl.ds(pl.multiple_of(r * z.seq, z.seq), z.seq), :] = RB[meta[at_ids + r]]

        for d in range(1, z.tps):
            scatter_copy(other_tp(d)).start()

    def sum_step():
        total = PH[piece(tp), :].astype(jnp.float32)
        for d in range(1, z.tps):
            c = other_tp(d)
            remote(PH.at[piece(c)], RSB.at[c], v["rss"].at[c], v["rsr"].at[c], (rep, c)).wait_recv()
            total = total + RSB[c].astype(jnp.float32)
        SH[piece(tp), :] = total.astype(jnp.bfloat16)
        for d in range(1, z.tps):
            gather_copy(other_tp(d)).start()

    def sum_finish():
        for d in range(1, z.tps):
            c = other_tp(d)
            remote(SH.at[piece(c)], SH.at[piece(c)], v["ags"].at[c], v["agr"].at[c], (rep, c)).wait_recv()

    def project(s, i, first):
        rows = chunk_rows(i)
        x = G[s, rows, :]
        wide = min(512, z.qcols)
        for n in range(0, z.qcols, wide):
            r = jnp.dot(
                x,
                W[pl.ds(pl.multiple_of(s * z.feat, z.feat), z.feat), n : n + wide],
                preferred_element_type=jnp.float32,
            )
            if first:
                ACC[rows, n : n + wide] = r
            else:
                ACC[rows, n : n + wide] += r

    heads = z.qcols // HEAD_SIZE
    cos = v["cosine"][...]
    sin = v["sine"][...]

    def rotate(x):
        return (x * cos + pltpu.roll(x, HALF, 1) * sin).astype(jnp.bfloat16)

    def attend_request(r):
        rows = pl.ds(pl.multiple_of(r * z.seq, z.seq), z.seq)
        table = meta[at_homes + r]
        size = meta[at_sizes + r]
        low = SH[rows, :]

        def change(side, up):
            d = jnp.dot(low[:, side * z.rank : (side + 1) * z.rank], up, preferred_element_type=jnp.float32)
            return (adapter_scale * d).astype(jnp.bfloat16).astype(jnp.float32)

        up_kv = UKV[table]
        base = PO[head, rows, :]
        keys_raw = (base[:, :HEAD_SIZE] + change(1, up_kv[:, :HEAD_SIZE])).astype(jnp.bfloat16)
        values = (base[:, HEAD_SIZE:] + change(2, up_kv[:, HEAD_SIZE:])).astype(jnp.bfloat16)
        keys = rotate(keys_raw.astype(jnp.float32))
        raw = ACC[rows, :] + change(0, UQ[table])
        query = jnp.concatenate(
            [rotate(raw[:, h * HEAD_SIZE : (h + 1) * HEAD_SIZE]) for h in range(heads)], axis=0
        )
        scores = nt_dot(keys, query) * (1.0 / math.sqrt(HEAD_SIZE))
        p_at = lax.broadcasted_iota(jnp.int32, scores.shape, 0)
        q_at = lax.broadcasted_iota(jnp.int32, scores.shape, 1) % z.seq
        scores = jnp.where((p_at <= q_at) & (p_at < size), scores, jnp.float32(-1e30))
        weights = jnp.exp(scores - jnp.max(scores, axis=0, keepdims=True))
        probs = (weights / jnp.sum(weights, axis=0, keepdims=True)).astype(jnp.bfloat16)
        mixed = lax.dot_general(
            probs, values, (((0,), (0,)), ((), ())), preferred_element_type=jnp.float32
        )
        live = lax.broadcasted_iota(jnp.int32, mixed.shape, 0) % z.seq < size
        mixed = jnp.where(live, mixed, 0.0).astype(jnp.bfloat16)
        for h in range(heads):
            OB[rows, h * HEAD_SIZE : (h + 1) * HEAD_SIZE] = mixed[h * z.seq : (h + 1) * z.seq]

    per_chunk = z.chunk // z.seq

    def out_copy(i):
        return pltpu.make_async_copy(OB.at[chunk_rows(i)], out.at[chunk_rows(i)], v["outs"].at[i])

    def attend(i):
        @pl.loop(0, per_chunk)
        def _(b):
            attend_request(i * per_chunk + b)

        out_copy(i).start()

    total_hooks = z.hooks
    first_attend = total_hooks - CHUNKS

    def scaled(x):
        return x * total_hooks // 24

    events = {}

    def add(at, what):
        events.setdefault(at, []).append(what)

    add(0, pair_sums)
    for n in range(last):
        add(scaled(1 + 2 * n) if z.tps <= 4 else 1 + 2 * n, lambda n=n: pair_step(n))
    add(scaled(8), shrink_step)
    add(scaled(10), home_step)
    add(scaled(12), sum_step)
    add(scaled(13), up_forward)
    add(first_attend - 1, up_finish)
    add(first_attend - 1, sum_finish)
    add(first_attend - 1, pair_finish)

    load_w.wait()

    @pl.loop(0, CHUNKS)
    def _(i):
        @pl.when(i + LEAD < CHUNKS)
        def _():
            send_own(i + LEAD)

        @pl.when(i >= 2)
        def _():
            for side in range(2):
                for d in range(0, last):
                    s = tp - d if side == 0 else tp + d
                    ok = (s >= 0) & (tp < last) if side == 0 else (s <= last) & (tp > 0)

                    @pl.when(ok)
                    def _():
                        hop(side, s, i - 2).wait_send()

        project(tp, i, True)
        for d in range(1, z.tps):
            for side in range(2):
                s = tp - d if side == 0 else tp + d
                ok = s >= 0 if side == 0 else s <= last
                on = ok & (tp < last) if side == 0 else ok & (tp > 0)

                @pl.when(ok)
                def _():
                    hop(side, s, i).wait_recv()

                @pl.when(on)
                def _():
                    hop(side, s, i).start()

            for side in range(2):
                s = tp - d if side == 0 else tp + d
                ok = s >= 0 if side == 0 else s <= last

                @pl.when(ok)
                def _():
                    project(s, i, False)

            for at in sorted(events):
                if at % last == d - 1:

                    @pl.when(i == at // last)
                    def _():
                        for what in events[at]:
                            what()

            h = i * last + (d - 1)

            @pl.when(h >= first_attend)
            def _():
                attend(h - first_attend)

    for side in range(2):
        for d in range(0, last):
            s = tp - d if side == 0 else tp + d
            ok = (s >= 0) & (tp < last) if side == 0 else (s <= last) & (tp > 0)

            @pl.when(ok)
            def _():
                for i in range(CHUNKS - 2, CHUNKS):
                    hop(side, s, i).wait_send()

    for c in range(z.tps):
        for side in range(2):
            owner, column = table_side(side, c)
            if owner != c:

                @pl.when(tp == owner)
                def _():
                    src = v["upkv"].at[:, :, pl.ds(column, HEAD_SIZE)]
                    remote(src, table_dst(side), v["uks"].at[side, c], v["ukr"].at[side], (rep, c)).wait_send()

        @pl.when(tp < c)
        def _():
            pair_hop(0, c).wait_send()

        @pl.when(tp > c)
        def _():
            pair_hop(1, c).wait_send()

    @pl.loop(1, z.reps)
    def _(k):
        return_copy(jnp.bitwise_xor(rep, k)).wait_send()

    for d in range(1, z.tps):
        scatter_copy(other_tp(d)).wait_send()
        gather_copy(other_tp(d)).wait_send()
    for k in range(0, z.reps, 2):
        if k:
            for c in peer_copies(k):
                c.wait_send()
        for c in sibling_copies(k):
            c.wait_send()
    for i in range(CHUNKS):
        out_copy(i).wait()


def fused(z, meta, marks, tokens, wq, wkv, down, upq, upkv):
    cosine, sine = rope_tables(z.seq)
    by_request = tokens.reshape(z.requests, z.seq, z.feat)
    bf16, f32 = jnp.bfloat16, jnp.float32
    V = pltpu.VMEM
    D = pltpu.SemaphoreType.DMA
    rows_q = z.cap * z.seq
    scratch = [
        V((z.requests, z.seq, z.feat), bf16),
        V((z.tps, z.rows, z.feat), bf16),
        V((z.tps * z.feat, z.qcols), bf16),
        V((z.feat, z.pcols), bf16),
        V((z.tables * z.outs, z.feat), bf16),
        V((z.reps, rows_q, z.feat), bf16),
        V((z.reps, rows_q, z.feat), bf16),
        V(marks.shape, f32),
        V((z.slots, z.seq, LOW), bf16),
        V((z.slots, z.seq, LOW), bf16),
        V((z.rows, LOW), bf16),
        V((z.tps, z.piece, LOW), bf16),
        V((z.rows, LOW), bf16),
        V((z.reps * z.tables, z.rank, z.qcols), bf16),
        V((z.reps * z.tables, z.rank, 2 * HEAD_SIZE), bf16),
        V((z.rows, z.qcols), f32),
        V((z.kv_heads, z.rows, 2 * HEAD_SIZE), f32),
        V((z.tps, z.rows, 2 * HEAD_SIZE), bf16),
        V((z.tps, z.rows, 2 * HEAD_SIZE), bf16),
        V((z.rows, z.qcols), bf16),
        D((6,)),
        D((CHUNKS,)),
        D((2, z.tps, CHUNKS)),
        D((2, z.tps, CHUNKS)),
        D((z.reps,)),
        D((z.reps,)),
        D((z.reps,)),
        D((z.reps,)),
        D((z.reps,)),
        D((z.reps,)),
        D((2, z.tps)),
        D((2, z.tps)),
        D((z.tps,)),
        D((z.tps,)),
        D((z.tps,)),
        D((z.tps,)),
        D((2, z.tps)),
        D((2,)),
        D((z.reps,)),
        D((z.reps,)),
        D((z.reps,)),
        D((z.reps,)),
        D((z.reps,)),
        D((z.reps,)),
    ]
    vmem = pl.BlockSpec(memory_space=pltpu.VMEM)
    smem = pl.BlockSpec(memory_space=pltpu.SMEM)
    hbm = pl.BlockSpec(memory_space=pl.ANY)
    flops = 2 * z.rows * z.feat * (z.tps * z.qcols + z.pcols)

    def body(*refs):
        fused_kernel(z, *refs)

    return pl.pallas_call(
        body,
        out_shape=jax.ShapeDtypeStruct((z.rows, z.qcols), bf16),
        in_specs=[smem, vmem, vmem, vmem] + [hbm] * 7,
        out_specs=hbm,
        scratch_shapes=scratch,
        compiler_params=pltpu.CompilerParams(
            collective_id=0, has_side_effects=True, vmem_limit_bytes=62 << 20
        ),
        cost_estimate=pl.CostEstimate(flops=flops, bytes_accessed=28 << 20, transcendentals=1 << 20),
    )(meta, marks, jnp.asarray(cosine), jnp.asarray(sine), tokens, by_request, wq, wkv, down, upq, upkv)


def shards(
    tokens,
    query_weight,
    key_value_weight,
    adapter_down_tables,
    adapter_up_query,
    adapter_up_key_value,
    request_adapter,
    request_token_length,
    adapter_table_row,
):
    tables, outs, feat = adapter_down_tables.shape
    z = Sizes(
        lax.axis_size("rep"),
        lax.axis_size("tp"),
        tokens.shape,
        query_weight.shape,
        key_value_weight.shape,
        tables,
        adapter_up_query.shape[1],
        request_adapter.shape[0],
        adapter_up_key_value.shape[2],
    )
    match = request_adapter[:, None] == jnp.arange(adapter_table_row.shape[0], dtype=jnp.int32)
    homes = jnp.sum(jnp.where(match, adapter_table_row[None, :], 0), axis=1)
    owners = homes // tables
    pos = jnp.arange(z.requests, dtype=jnp.int32)
    earlier = (owners[:, None] == owners[None, :]) & (pos[None, :] < pos[:, None])
    slot_ids = owners * z.cap + jnp.sum(earlier.astype(jnp.int32), axis=1)
    slot_at = jnp.arange(z.slots, dtype=jnp.int32)
    taken = slot_ids[None, :] == slot_at[:, None]
    picks = jnp.sum(jnp.where(taken, pos, 0), axis=1)
    slot_local = jnp.sum(jnp.where(taken, (homes % tables)[None, :], 0), axis=1)
    meta = jnp.concatenate([picks, slot_ids, homes, request_token_length]).astype(jnp.int32)
    mark_rows = -(-z.cap // 8) * 8
    marks = jnp.pad(slot_local.astype(jnp.float32).reshape(z.reps, z.cap), ((0, 0), (0, mark_rows - z.cap)))
    marks = jnp.broadcast_to(marks[:, :, None], (z.reps, mark_rows, 128))
    return fused(
        z,
        meta,
        marks,
        tokens,
        query_weight,
        key_value_weight,
        adapter_down_tables.reshape(tables * outs, feat),
        adapter_up_query,
        adapter_up_key_value,
    )


def solution(mesh):
    placed = (
        P("rep", "tp"),
        P(None, "tp"),
        P("tp", None),
        P("rep", None, "tp"),
        P("rep", None, "tp"),
        P("rep", None, "tp"),
        P("rep"),
        P("rep"),
        P(),
    )
    return jax.shard_map(
        shards, mesh=mesh, in_specs=placed, out_specs=P("rep", "tp"), check_vma=False
    )
```

```python
import math

import jax
import jax.numpy as jnp
import numpy as np
from jax import lax
from jax.experimental import pallas as pl
from jax.experimental.pallas import tpu as pltpu
from jax.sharding import PartitionSpec as P

HEAD_SIZE = 128
HALF = HEAD_SIZE // 2
SIDES = 3
LOW = 256
CHUNKS = 8
LEAD = 2
TAIL = 3
SKEW = 1

adapter_scale = 0.5
rope_theta = 500000.0
MESH = pl.DeviceIdType.MESH


def rope_tables(seq_len):
    frequency = np.float64(rope_theta) ** (-(np.arange(HALF, dtype=np.float64) * 2.0 / HEAD_SIZE))
    angles = np.arange(seq_len).astype(np.float64)[:, None] * frequency[None, :]
    cosine = np.concatenate([np.cos(angles), np.cos(angles)], axis=1)
    sine = np.concatenate([-np.sin(angles), np.sin(angles)], axis=1)
    return cosine.astype(np.float32), sine.astype(np.float32)


def nt_dot(a, b):
    return lax.dot_general(a, b, (((1,), (1,)), ((), ())), preferred_element_type=jnp.float32)


class Sizes:
    def __init__(self, replicas, tps, tokens, wq, wkv, tables, rank, requests, portion):
        self.reps = replicas
        self.tps = tps
        self.rows, self.feat = tokens
        self.qcols = wq[1]
        self.pcols = wkv[1]
        self.tables = tables
        self.rank = rank
        self.outs = SIDES * rank
        self.requests = requests
        self.seq = self.rows // requests
        self.cap = max(1, 2 * requests // replicas)
        self.slots = self.cap * replicas
        self.kv_heads = self.pcols // (2 * HEAD_SIZE)
        self.sharing = tps // self.kv_heads
        self.portion = portion
        self.chunk = self.rows // CHUNKS
        self.piece = self.rows // tps
        self.rounds = CHUNKS + (tps - 2) * SKEW
        self.hooks = self.rounds * (tps - 1)


def fused_kernel(z, *refs):
    names = (
        "meta", "marks", "cosine", "sine", "tokens", "by_request", "wq", "wkv", "down", "upq",
        "upkv", "out", "T", "G", "W", "WKV", "DN", "S", "RX", "MR", "SR", "RB", "PH", "RSB", "SH",
        "UQ", "UKV", "ACC", "PO", "CR", "CL", "OB", "WX", "PX", "loc", "outs", "gs", "gr", "as_", "ar", "ms",
        "mr", "ts", "tr", "cs", "cr", "rss", "rsr", "ags", "agr", "uks", "ukr", "uqs", "uqr",
        "uqf", "ves", "ver", "vef", "xs", "xr", "xps", "xpf", "pxs", "pxr",
    )
    v = dict(zip(names, refs))
    meta, marks, tokens, out = v["meta"], v["marks"], v["tokens"], v["out"]
    G, W, WKV, DN, S, RX, MR, SR, RB = (v[n] for n in names[names.index("G") : names.index("PH")])
    PH, RSB, SH, UQ, UKV, ACC, PO, CR, CL, OB, WX, PX = (
        v[n] for n in names[names.index("PH") : names.index("loc")]
    )
    loc = v["loc"]
    rep = lax.axis_index("rep")
    tp = lax.axis_index("tp")
    last = z.tps - 1
    head = tp // z.sharing
    at_slots, at_ids, at_homes, at_sizes = 0, z.slots, z.slots + z.requests, z.slots + 2 * z.requests

    def remote(src, dst, send, recv, to):
        return pltpu.make_async_remote_copy(
            src_ref=src, dst_ref=dst, send_sem=send, recv_sem=recv, device_id=to, device_id_type=MESH
        )

    def other_tp(d):
        return lax.rem(tp + d, z.tps)

    T = v["T"]
    load_tokens = pltpu.make_async_copy(tokens, G.at[tp], loc.at[0])
    load_requests = pltpu.make_async_copy(v["by_request"], T, loc.at[5])
    load_wkv = pltpu.make_async_copy(v["wkv"], WKV, loc.at[1])
    load_w = pltpu.make_async_copy(v["wq"], W, loc.at[2])
    load_down = pltpu.make_async_copy(v["down"], DN, loc.at[3])
    my_tables = pl.ds(rep * z.tables, z.tables)
    load_upq = pltpu.make_async_copy(v["upq"], UQ.at[my_tables], loc.at[4])
    for c in (load_tokens, load_requests):
        c.start()

    barrier = pltpu.get_barrier_semaphore()
    for k in range(1, z.reps):
        pl.semaphore_signal(barrier, inc=1, device_id=(jnp.bitwise_xor(rep, k), tp), device_id_type=MESH)
    for d in range(1, z.tps):
        pl.semaphore_signal(barrier, inc=1, device_id=(rep, other_tp(d)), device_id_type=MESH)
    pl.semaphore_wait(barrier, z.reps - 1 + z.tps - 1)

    def chunk_rows(i):
        return pl.ds(pl.multiple_of(i * z.chunk, z.chunk), z.chunk)

    def hop(side, s, i):
        to = lax.rem(tp + 1, z.tps) if side == 0 else lax.rem(tp + last, z.tps)
        part = G.at[s, chunk_rows(i)]
        return remote(part, part, v["gs"].at[side, s, i], v["gr"].at[side, s, i], (rep, to))

    is_end = (tp == 0) | (tp == last)
    is_helper = (tp == 1) | (tp == last - 1)

    def comes(side, d):
        s = tp - d if side == 0 else tp + d
        inside = s >= 0 if side == 0 else s <= last
        return s, inside & ~is_end if d == 1 else inside

    def goes(side, d):
        s = tp - d if side == 0 else tp + d
        if side == 0:
            ok = (s >= 0) & (tp < last)
            return s, ok & (tp != last - 1) if d == 0 else ok & comes(0, d)[1]
        ok = (s <= last) & (tp > 0)
        return s, ok & (tp != 1) if d == 0 else ok & comes(1, d)[1]

    def send_own(i):
        for side in range(2):

            @pl.when(goes(side, 0)[1])
            def _():
                hop(side, tp, i).start()

    share = z.feat // z.reps

    def weight_share(q):
        return WX.at[pl.ds(pl.multiple_of(q * share, share), share)]

    def weight_copy():
        helper = jnp.where(tp == 0, 1, last - 1)
        at = pl.multiple_of(helper * z.feat + rep * share, share)
        return remote(
            v["wq"].at[pl.ds(at, share)], weight_share(rep), v["xs"].at[0], v["xr"].at[rep], (rep, helper)
        )

    def weight_peer(k):
        part = weight_share(rep)
        return remote(part, part, v["xps"].at[k], v["xr"].at[rep], (jnp.bitwise_xor(rep, k), tp))

    def weight_sibling(k):
        q = jnp.bitwise_xor(rep, k)
        part = weight_share(q)
        return remote(part, part, v["xpf"].at[k], v["xr"].at[q], (jnp.bitwise_xor(rep, 1), tp))

    def weight_arrives(q):
        part = weight_share(q)
        remote(part, part, v["xs"].at[0], v["xr"].at[q], (q, tp)).wait_recv()

    def weight_send():
        @pl.when(is_helper)
        def _():
            weight_arrives(rep)
            for k in range(2, z.reps, 2):
                weight_peer(k).start()
            weight_sibling(0).start()

    def weight_forward():
        @pl.when(is_helper)
        def _():
            for k in range(2, z.reps, 2):
                weight_arrives(jnp.bitwise_xor(rep, k))
                weight_sibling(k).start()

    def weight_finish():
        @pl.when(is_helper)
        def _():
            for k in range(1, z.reps, 2):
                weight_arrives(jnp.bitwise_xor(rep, k))

    def partial_copy(i):
        part = PX.at[chunk_rows(i)]
        end = jnp.where(tp == 1, 0, last)
        return remote(part, part, v["pxs"].at[i], v["pxr"].at[i], (rep, end))

    def partial(i):
        rows = chunk_rows(i)
        wide = min(512, z.qcols)
        for n in range(0, z.qcols, wide):
            r = jnp.dot(G[tp, rows, :], WX[:, n : n + wide], preferred_element_type=jnp.float32)
            PX[rows, n : n + wide] = r.astype(jnp.bfloat16)
        partial_copy(i).start()

    def take_partial(i):
        @pl.when(is_end)
        def _():
            rows = chunk_rows(i)
            partial_copy(i).wait_recv()
            ACC[rows, :] += PX[rows, :].astype(jnp.float32)

    def table_side(side, c):
        column = (c // z.sharing) * HEAD_SIZE + side * z.kv_heads * HEAD_SIZE
        return column // z.portion, column % z.portion

    def table_dst(side):
        return UKV.at[my_tables, :, pl.ds(side * HEAD_SIZE, HEAD_SIZE)]

    for c in range(z.tps):
        for side in range(2):
            owner, column = table_side(side, c)
            src = v["upkv"].at[:, :, pl.ds(column, HEAD_SIZE)]
            if owner == c:

                @pl.when(tp == c)
                def _():
                    pltpu.make_async_copy(src, table_dst(side), v["ukr"].at[side]).start()

            else:

                @pl.when(tp == owner)
                def _():
                    remote(src, table_dst(side), v["uks"].at[side, c], v["ukr"].at[side], (rep, c)).start()

    load_tokens.wait()
    for c in (load_wkv, load_w, load_down, load_upq):
        c.start()
    send_own(0)

    @pl.when(is_end)
    def _():
        weight_copy().start()

    for i in range(1, LEAD):
        send_own(i)

    def group(q):
        return pl.ds(q * z.cap, z.cap)

    def pack(q, dst):
        for j in range(z.cap):
            pick = meta[at_slots + q * z.cap + j]
            dst[q, j * z.seq : (j + 1) * z.seq, :] = T[pick]

    def token_copy(q):
        return remote(S.at[q], RX.at[rep], v["as_"].at[q], v["ar"].at[rep], (q, tp))

    def mark_copy(q):
        return remote(marks.at[q], MR.at[rep], v["ms"].at[q], v["mr"].at[rep], (q, tp))

    def return_copy(q):
        return remote(SR.at[group(q)], RB.at[group(rep)], v["ts"].at[q], v["tr"].at[rep], (q, tp))

    load_requests.wait()

    @pl.loop(1, z.reps)
    def _(k):
        q = jnp.bitwise_xor(rep, k)
        pack(q, S)
        token_copy(q).start()
        mark_copy(q).start()

    pack(rep, RX)
    MR[rep] = marks[rep]

    def pair_sums():
        load_wkv.wait()
        half = z.kv_heads * HEAD_SIZE

        @pl.loop(0, z.rows // 128)
        def _(b):
            rows = pl.ds(pl.multiple_of(b * 128, 128), 128)
            x = G[tp, rows, :]
            for side in range(2):
                r = jnp.dot(x, WKV[:, side * half : (side + 1) * half], preferred_element_type=jnp.float32)
                for h in range(z.kv_heads):
                    PO[h, rows, side * HEAD_SIZE : (side + 1) * HEAD_SIZE] = r[
                        :, h * HEAD_SIZE : (h + 1) * HEAD_SIZE
                    ]

    def pair_hop(side, c):
        to = lax.rem(tp + 1, z.tps) if side == 0 else lax.rem(tp + last, z.tps)
        buf = (CR if side == 0 else CL).at[c]
        return remote(buf, buf, v["cs"].at[side, c], v["cr"].at[side, c], (rep, to))

    def pair_step(n):
        for c in reversed(range(z.tps)):
            if c > n:

                @pl.when(tp == n)
                def _():
                    own = PO[c // z.sharing]
                    if n > 0:
                        pair_hop(0, c).wait_recv()
                        own = own + CR[c].astype(jnp.float32)
                    CR[c] = own.astype(jnp.bfloat16)
                    pair_hop(0, c).start()

        for c in range(z.tps):
            if c < last - n:

                @pl.when(tp == last - n)
                def _():
                    own = PO[c // z.sharing]
                    if n > 0:
                        pair_hop(1, c).wait_recv()
                        own = own + CL[c].astype(jnp.float32)
                    CL[c] = own.astype(jnp.bfloat16)
                    pair_hop(1, c).start()

    def pair_finish():
        @pl.when(tp > 0)
        def _():
            pair_hop(0, tp).wait_recv()
            PO[head] = PO[head] + CR[tp].astype(jnp.float32)

        @pl.when(tp < last)
        def _():
            pair_hop(1, tp).wait_recv()
            PO[head] = PO[head] + CL[tp].astype(jnp.float32)

    def shrink_of(q):
        x = RX[q]
        parts = [nt_dot(x, DN[a * z.outs : (a + 1) * z.outs, :]) for a in range(z.tables)]
        for j in range(z.cap):
            mark = MR[q, j : j + 1, 0:1]
            total = jnp.zeros((z.seq, z.outs), jnp.float32)
            for a in range(z.tables):
                total = jnp.where(mark == float(a), parts[a][j * z.seq : (j + 1) * z.seq], total)
            low = jnp.concatenate([total, jnp.zeros((z.seq, LOW - z.outs), jnp.float32)], axis=1)
            SR[q * z.cap + j] = low.astype(jnp.bfloat16)

    def up_copies(q, source, send_q, send_v):
        part = pl.ds(source * z.tables, z.tables)
        return (
            remote(UQ.at[part], UQ.at[part], send_q, v["uqr"].at[source], (q, tp)),
            remote(UKV.at[part], UKV.at[part], send_v, v["ver"].at[source], (q, tp)),
        )

    def peer_copies(k):
        q = jnp.bitwise_xor(rep, k)
        return up_copies(q, rep, v["uqs"].at[k], v["ves"].at[k])

    def sibling_copies(k):
        return up_copies(jnp.bitwise_xor(rep, 1), jnp.bitwise_xor(rep, k), v["uqf"].at[k], v["vef"].at[k])

    def shrink_step(lo, hi):
        if lo == 0:
            load_down.wait()

        @pl.loop(lo, hi)
        def _(k):
            q = jnp.bitwise_xor(rep, k)

            @pl.when(k > 0)
            def _():
                token_copy(q).wait_send()
                mark_copy(q).wait_send()
                remote(S.at[q], RX.at[q], v["as_"].at[q], v["ar"].at[q], (q, tp)).wait_recv()
                remote(marks.at[q], MR.at[q], v["ms"].at[q], v["mr"].at[q], (q, tp)).wait_recv()

            shrink_of(q)

            @pl.when(k > 0)
            def _():
                return_copy(q).start()

            @pl.when(k == 0)
            def _():
                RB[group(rep)] = SR[group(rep)]

    def up_send():
        load_upq.wait()
        for side in range(2):
            pltpu.make_async_copy(table_dst(side), table_dst(side), v["ukr"].at[side]).wait()
        for k in range(2, z.reps, 2):
            for c in peer_copies(k):
                c.start()
        for c in sibling_copies(0):
            c.start()

    def up_forward():
        for k in range(2, z.reps, 2):
            q = jnp.bitwise_xor(rep, k)
            for c in up_copies(q, q, v["uqs"].at[k], v["ves"].at[k]):
                c.wait_recv()
            for c in sibling_copies(k):
                c.start()

    def up_finish():
        for k in range(0, z.reps, 2):
            q = jnp.bitwise_xor(rep, k + 1)
            for c in up_copies(q, q, v["uqf"].at[k], v["vef"].at[k]):
                c.wait_recv()

    def piece(c):
        return pl.ds(pl.multiple_of(c * z.piece, z.piece), z.piece)

    def scatter_copy(c):
        return remote(PH.at[piece(c)], RSB.at[tp], v["rss"].at[c], v["rsr"].at[tp], (rep, c))

    def gather_copy(c):
        return remote(SH.at[piece(tp)], SH.at[piece(tp)], v["ags"].at[c], v["agr"].at[tp], (rep, c))

    def home_step():
        @pl.loop(1, z.reps)
        def _(k):
            q = jnp.bitwise_xor(rep, k)
            remote(SR.at[group(q)], RB.at[group(q)], v["ts"].at[q], v["tr"].at[q], (q, tp)).wait_recv()

        @pl.loop(0, z.requests)
        def _(r):
            PH[pl.ds(pl.multiple_of(r * z.seq, z.seq), z.seq), :] = RB[meta[at_ids + r]]

        for d in range(1, z.tps):
            scatter_copy(other_tp(d)).start()

    def sum_step():
        total = PH[piece(tp), :].astype(jnp.float32)
        for d in range(1, z.tps):
            c = other_tp(d)
            remote(PH.at[piece(c)], RSB.at[c], v["rss"].at[c], v["rsr"].at[c], (rep, c)).wait_recv()
            total = total + RSB[c].astype(jnp.float32)
        SH[piece(tp), :] = total.astype(jnp.bfloat16)
        for d in range(1, z.tps):
            gather_copy(other_tp(d)).start()

    def sum_finish():
        for d in range(1, z.tps):
            c = other_tp(d)
            remote(SH.at[piece(c)], SH.at[piece(c)], v["ags"].at[c], v["agr"].at[c], (rep, c)).wait_recv()

    def project(s, i, first):
        rows = chunk_rows(i)
        x = G[s, rows, :]
        wide = min(512, z.qcols)
        for n in range(0, z.qcols, wide):
            r = jnp.dot(
                x,
                W[pl.ds(pl.multiple_of(s * z.feat, z.feat), z.feat), n : n + wide],
                preferred_element_type=jnp.float32,
            )
            if first:
                ACC[rows, n : n + wide] = r
            else:
                ACC[rows, n : n + wide] += r

    heads = z.qcols // HEAD_SIZE
    cos = v["cosine"][...]
    sin = v["sine"][...]

    def rotate(x):
        return (x * cos + pltpu.roll(x, HALF, 1) * sin).astype(jnp.bfloat16)

    def attend_request(r):
        rows = pl.ds(pl.multiple_of(r * z.seq, z.seq), z.seq)
        table = meta[at_homes + r]
        size = meta[at_sizes + r]
        low = SH[rows, :]

        def change(side, up):
            d = jnp.dot(low[:, side * z.rank : (side + 1) * z.rank], up, preferred_element_type=jnp.float32)
            return (adapter_scale * d).astype(jnp.bfloat16).astype(jnp.float32)

        up_kv = UKV[table]
        base = PO[head, rows, :]
        keys_raw = (base[:, :HEAD_SIZE] + change(1, up_kv[:, :HEAD_SIZE])).astype(jnp.bfloat16)
        values = (base[:, HEAD_SIZE:] + change(2, up_kv[:, HEAD_SIZE:])).astype(jnp.bfloat16)
        keys = rotate(keys_raw.astype(jnp.float32))
        raw = ACC[rows, :] + change(0, UQ[table])
        query = jnp.concatenate(
            [rotate(raw[:, h * HEAD_SIZE : (h + 1) * HEAD_SIZE]) for h in range(heads)], axis=0
        )
        scores = nt_dot(keys, query) * (1.0 / math.sqrt(HEAD_SIZE))
        p_at = lax.broadcasted_iota(jnp.int32, scores.shape, 0)
        q_at = lax.broadcasted_iota(jnp.int32, scores.shape, 1) % z.seq
        scores = jnp.where((p_at <= q_at) & (p_at < size), scores, jnp.float32(-1e30))
        weights = jnp.exp(scores - jnp.max(scores, axis=0, keepdims=True))
        probs = (weights / jnp.sum(weights, axis=0, keepdims=True)).astype(jnp.bfloat16)
        mixed = lax.dot_general(
            probs, values, (((0,), (0,)), ((), ())), preferred_element_type=jnp.float32
        )
        live = lax.broadcasted_iota(jnp.int32, mixed.shape, 0) % z.seq < size
        mixed = jnp.where(live, mixed, 0.0).astype(jnp.bfloat16)
        for h in range(heads):
            OB[rows, h * HEAD_SIZE : (h + 1) * HEAD_SIZE] = mixed[h * z.seq : (h + 1) * z.seq]

    per_chunk = z.chunk // z.seq

    def out_copy(i):
        return pltpu.make_async_copy(OB.at[chunk_rows(i)], out.at[chunk_rows(i)], v["outs"].at[i])

    def attend(lo, hi):
        @pl.loop(lo, hi)
        def _(i):
            take_partial(i)

            @pl.loop(0, per_chunk)
            def _(b):
                attend_request(i * per_chunk + b)

            out_copy(i).start()

    total_hooks = z.hooks

    def scaled(x):
        return x * total_hooks // 30

    first_partial = scaled(17)
    events = {}

    def add(at, what):
        events.setdefault(at, []).append(what)

    add(0, pair_sums)
    for n in range(last):
        add(scaled(3 + 8 * n // (last - 1)), lambda n=n: pair_step(n))
    add(scaled(3), weight_send)
    per_hook = -(-z.reps // 8)
    for j in range(8):
        add(scaled(13) + j, lambda lo=j * per_hook: shrink_step(lo, min(z.reps, lo + per_hook)))
    add(scaled(13), weight_forward)
    add(first_partial, weight_finish)
    add(scaled(17), up_send)
    add(scaled(21), home_step)
    add(scaled(23), sum_step)
    add(scaled(25), pair_finish)
    add(scaled(25), up_forward)
    add(total_hooks - TAIL, up_finish)
    add(total_hooks - TAIL, sum_finish)
    step = -(-(CHUNKS - 1) // (TAIL - 1))
    for j in range(TAIL - 1):
        lo, hi = j * step, min(CHUNKS - 1, j * step + step)
        add(total_hooks - TAIL + j, lambda lo=lo, hi=hi: attend(lo, hi))
    add(total_hooks - 1, lambda: attend(CHUNKS - 1, CHUNKS))

    @pl.loop(0, z.rounds)
    def _(i):
        for d in range(1, z.tps):
            j = i - (d - 1) * SKEW

            @pl.when((j >= 0) & (j < CHUNKS))
            def _():
                for side in range(2):
                    s, ok = comes(side, d)

                    @pl.when(ok)
                    def _():
                        hop(side, s, j).wait_recv()

                    @pl.when(goes(side, d)[1])
                    def _():
                        hop(side, s, j).start()

                if d == 1:

                    @pl.when(i + LEAD < CHUNKS)
                    def _():
                        send_own(i + LEAD)

                    @pl.when(i == 0)
                    def _():
                        load_w.wait()

                    project(tp, j, True)
                for side in range(2):
                    s, ok = comes(side, d)

                    @pl.when(ok)
                    def _():
                        project(s, j, False)

            h = i * last + (d - 1)
            for at in sorted(events):
                if at % last == d - 1:

                    @pl.when(i == at // last)
                    def _():
                        for what in events[at]:
                            what()

            @pl.when((h >= first_partial) & (h < first_partial + CHUNKS) & is_helper)
            def _():
                partial(h - first_partial)

    for side in range(2):
        for d in range(0, last):
            s, ok = goes(side, d)

            @pl.when(ok)
            def _():
                @pl.loop(0, CHUNKS)
                def _(i):
                    hop(side, s, i).wait_send()

    @pl.when(is_end)
    def _():
        weight_copy().wait_send()

    @pl.when(is_helper)
    def _():
        for k in range(0, z.reps, 2):
            if k:
                weight_peer(k).wait_send()
            weight_sibling(k).wait_send()
        for i in range(CHUNKS):
            partial_copy(i).wait_send()

    for c in range(z.tps):
        for side in range(2):
            owner, column = table_side(side, c)
            if owner != c:

                @pl.when(tp == owner)
                def _():
                    src = v["upkv"].at[:, :, pl.ds(column, HEAD_SIZE)]
                    remote(src, table_dst(side), v["uks"].at[side, c], v["ukr"].at[side], (rep, c)).wait_send()

        @pl.when(tp < c)
        def _():
            pair_hop(0, c).wait_send()

        @pl.when(tp > c)
        def _():
            pair_hop(1, c).wait_send()

    @pl.loop(1, z.reps)
    def _(k):
        return_copy(jnp.bitwise_xor(rep, k)).wait_send()

    for d in range(1, z.tps):
        scatter_copy(other_tp(d)).wait_send()
        gather_copy(other_tp(d)).wait_send()
    for k in range(0, z.reps, 2):
        if k:
            for c in peer_copies(k):
                c.wait_send()
        for c in sibling_copies(k):
            c.wait_send()
    for i in range(CHUNKS):
        out_copy(i).wait()


def fused(z, meta, marks, tokens, wq, wkv, down, upq, upkv):
    cosine, sine = rope_tables(z.seq)
    by_request = tokens.reshape(z.requests, z.seq, z.feat)
    bf16, f32 = jnp.bfloat16, jnp.float32
    V = pltpu.VMEM
    D = pltpu.SemaphoreType.DMA
    rows_q = z.cap * z.seq
    scratch = [
        V((z.requests, z.seq, z.feat), bf16),
        V((z.tps, z.rows, z.feat), bf16),
        V((z.tps * z.feat, z.qcols), bf16),
        V((z.feat, z.pcols), bf16),
        V((z.tables * z.outs, z.feat), bf16),
        V((z.reps, rows_q, z.feat), bf16),
        V((z.reps, rows_q, z.feat), bf16),
        V(marks.shape, f32),
        V((z.slots, z.seq, LOW), bf16),
        V((z.slots, z.seq, LOW), bf16),
        V((z.rows, LOW), bf16),
        V((z.tps, z.piece, LOW), bf16),
        V((z.rows, LOW), bf16),
        V((z.reps * z.tables, z.rank, z.qcols), bf16),
        V((z.reps * z.tables, z.rank, 2 * HEAD_SIZE), bf16),
        V((z.rows, z.qcols), f32),
        V((z.kv_heads, z.rows, 2 * HEAD_SIZE), f32),
        V((z.tps, z.rows, 2 * HEAD_SIZE), bf16),
        V((z.tps, z.rows, 2 * HEAD_SIZE), bf16),
        V((z.rows, z.qcols), bf16),
        V((z.feat, z.qcols), bf16),
        V((z.rows, z.qcols), bf16),
        D((6,)),
        D((CHUNKS,)),
        D((2, z.tps, CHUNKS)),
        D((2, z.tps, CHUNKS)),
        D((z.reps,)),
        D((z.reps,)),
        D((z.reps,)),
        D((z.reps,)),
        D((z.reps,)),
        D((z.reps,)),
        D((2, z.tps)),
        D((2, z.tps)),
        D((z.tps,)),
        D((z.tps,)),
        D((z.tps,)),
        D((z.tps,)),
        D((2, z.tps)),
        D((2,)),
        D((z.reps,)),
        D((z.reps,)),
        D((z.reps,)),
        D((z.reps,)),
        D((z.reps,)),
        D((z.reps,)),
        D((1,)),
        D((z.reps,)),
        D((z.reps,)),
        D((z.reps,)),
        D((CHUNKS,)),
        D((CHUNKS,)),
    ]
    vmem = pl.BlockSpec(memory_space=pltpu.VMEM)
    smem = pl.BlockSpec(memory_space=pltpu.SMEM)
    hbm = pl.BlockSpec(memory_space=pl.ANY)
    flops = 2 * z.rows * z.feat * (z.tps * z.qcols + z.pcols)

    def body(*refs):
        fused_kernel(z, *refs)

    return pl.pallas_call(
        body,
        out_shape=jax.ShapeDtypeStruct((z.rows, z.qcols), bf16),
        in_specs=[smem, vmem, vmem, vmem] + [hbm] * 7,
        out_specs=hbm,
        scratch_shapes=scratch,
        compiler_params=pltpu.CompilerParams(
            collective_id=0, has_side_effects=True, vmem_limit_bytes=62 << 20
        ),
        cost_estimate=pl.CostEstimate(flops=flops, bytes_accessed=28 << 20, transcendentals=1 << 20),
    )(meta, marks, jnp.asarray(cosine), jnp.asarray(sine), tokens, by_request, wq, wkv, down, upq, upkv)


def shards(
    tokens,
    query_weight,
    key_value_weight,
    adapter_down_tables,
    adapter_up_query,
    adapter_up_key_value,
    request_adapter,
    request_token_length,
    adapter_table_row,
):
    tables, outs, feat = adapter_down_tables.shape
    z = Sizes(
        lax.axis_size("rep"),
        lax.axis_size("tp"),
        tokens.shape,
        query_weight.shape,
        key_value_weight.shape,
        tables,
        adapter_up_query.shape[1],
        request_adapter.shape[0],
        adapter_up_key_value.shape[2],
    )
    match = request_adapter[:, None] == jnp.arange(adapter_table_row.shape[0], dtype=jnp.int32)
    homes = jnp.sum(jnp.where(match, adapter_table_row[None, :], 0), axis=1)
    owners = homes // tables
    pos = jnp.arange(z.requests, dtype=jnp.int32)
    earlier = (owners[:, None] == owners[None, :]) & (pos[None, :] < pos[:, None])
    slot_ids = owners * z.cap + jnp.sum(earlier.astype(jnp.int32), axis=1)
    slot_at = jnp.arange(z.slots, dtype=jnp.int32)
    taken = slot_ids[None, :] == slot_at[:, None]
    picks = jnp.sum(jnp.where(taken, pos, 0), axis=1)
    slot_local = jnp.sum(jnp.where(taken, (homes % tables)[None, :], 0), axis=1)
    meta = jnp.concatenate([picks, slot_ids, homes, request_token_length]).astype(jnp.int32)
    mark_rows = -(-z.cap // 8) * 8
    marks = jnp.pad(slot_local.astype(jnp.float32).reshape(z.reps, z.cap), ((0, 0), (0, mark_rows - z.cap)))
    marks = jnp.broadcast_to(marks[:, :, None], (z.reps, mark_rows, 128))
    return fused(
        z,
        meta,
        marks,
        tokens,
        query_weight,
        key_value_weight,
        adapter_down_tables.reshape(tables * outs, feat),
        adapter_up_query,
        adapter_up_key_value,
    )


def solution(mesh):
    placed = (
        P("rep", "tp"),
        P(None, "tp"),
        P("tp", None),
        P("rep", None, "tp"),
        P("rep", None, "tp"),
        P("rep", None, "tp"),
        P("rep"),
        P("rep"),
        P(),
    )
    return jax.shard_map(
        shards, mesh=mesh, in_specs=placed, out_specs=P("rep", "tp"), check_vma=False
    )
```

```python
import math

import jax
import jax.numpy as jnp
import numpy as np
from jax import lax
from jax.experimental import pallas as pl
from jax.experimental.pallas import tpu as pltpu
from jax.sharding import PartitionSpec as P

HEAD_SIZE = 128
HALF = HEAD_SIZE // 2
SIDES = 3
LOW = 256
CHUNKS = 8
LEAD = 2
TAIL = 3
WHOLE = 2
SKEW = 1

adapter_scale = 0.5
rope_theta = 500000.0
MESH = pl.DeviceIdType.MESH


def rope_tables(seq_len):
    frequency = np.float64(rope_theta) ** (-(np.arange(HALF, dtype=np.float64) * 2.0 / HEAD_SIZE))
    angles = np.arange(seq_len).astype(np.float64)[:, None] * frequency[None, :]
    cosine = np.concatenate([np.cos(angles), np.cos(angles)], axis=1)
    sine = np.concatenate([-np.sin(angles), np.sin(angles)], axis=1)
    return cosine.astype(np.float32), sine.astype(np.float32)


def nt_dot(a, b):
    return lax.dot_general(a, b, (((1,), (1,)), ((), ())), preferred_element_type=jnp.float32)


class Sizes:
    def __init__(self, replicas, tps, tokens, wq, wkv, tables, rank, requests, portion):
        self.reps = replicas
        self.tps = tps
        self.rows, self.feat = tokens
        self.qcols = wq[1]
        self.pcols = wkv[1]
        self.tables = tables
        self.rank = rank
        self.outs = SIDES * rank
        self.requests = requests
        self.seq = self.rows // requests
        self.cap = max(1, 2 * requests // replicas)
        self.slots = self.cap * replicas
        self.kv_heads = self.pcols // (2 * HEAD_SIZE)
        self.sharing = tps // self.kv_heads
        self.portion = portion
        self.chunk = self.rows // CHUNKS
        self.piece = self.rows // tps
        self.rounds = CHUNKS + (tps - 2) * SKEW
        self.hooks = self.rounds * (tps - 1)


def fused_kernel(z, *refs):
    names = (
        "meta", "cosine", "sine", "tokens", "by_request", "wq", "wkv", "down", "upq",
        "upkv", "out", "T", "G", "W", "WKV", "DN", "S", "RX", "MR", "SR", "RB", "PH", "RSB", "SH",
        "UQ", "UKV", "ACC", "PO", "CR", "CL", "OB", "WX", "PX", "MK", "loc", "outs", "gs", "gr", "as_", "ar", "ms",
        "mr", "ts", "tr", "cs", "cr", "rss", "rsr", "ags", "agr", "uks", "ukr", "uqs", "uqr",
        "uqf", "ves", "ver", "vef", "xs", "xr", "xps", "xpf", "pxs", "pxr",
    )
    v = dict(zip(names, refs))
    meta, tokens, out = v["meta"], v["tokens"], v["out"]
    G, W, WKV, DN, S, RX, MR, SR, RB = (v[n] for n in names[names.index("G") : names.index("PH")])
    PH, RSB, SH, UQ, UKV, ACC, PO, CR, CL, OB, WX, PX, MK = (
        v[n] for n in names[names.index("PH") : names.index("loc")]
    )
    loc = v["loc"]
    rep = lax.axis_index("rep")
    tp = lax.axis_index("tp")
    last = z.tps - 1
    head = tp // z.sharing
    at_slots, at_marks, at_ids = 0, z.slots, 2 * z.slots
    at_homes, at_sizes = at_ids + z.requests, at_ids + 2 * z.requests

    def remote(src, dst, send, recv, to):
        return pltpu.make_async_remote_copy(
            src_ref=src, dst_ref=dst, send_sem=send, recv_sem=recv, device_id=to, device_id_type=MESH
        )

    def other_tp(d):
        return lax.rem(tp + d, z.tps)

    T = v["T"]
    load_tokens = pltpu.make_async_copy(tokens, G.at[tp], loc.at[0])
    load_requests = pltpu.make_async_copy(v["by_request"], T, loc.at[5])
    load_wkv = pltpu.make_async_copy(v["wkv"], WKV, loc.at[1])
    load_w = pltpu.make_async_copy(v["wq"], W, loc.at[2])
    load_down = pltpu.make_async_copy(v["down"], DN, loc.at[3])
    my_tables = pl.ds(rep * z.tables, z.tables)
    load_upq = pltpu.make_async_copy(v["upq"], UQ.at[my_tables], loc.at[4])
    for c in (load_tokens, load_requests):
        c.start()

    barrier = pltpu.get_barrier_semaphore()
    for k in range(1, z.reps):
        pl.semaphore_signal(barrier, inc=1, device_id=(jnp.bitwise_xor(rep, k), tp), device_id_type=MESH)
    for d in range(1, z.tps):
        pl.semaphore_signal(barrier, inc=1, device_id=(rep, other_tp(d)), device_id_type=MESH)
    pl.semaphore_wait(barrier, z.reps - 1 + z.tps - 1)

    def chunk_rows(i):
        return pl.ds(pl.multiple_of(i * z.chunk, z.chunk), z.chunk)

    def hop(side, s, i):
        to = lax.rem(tp + 1, z.tps) if side == 0 else lax.rem(tp + last, z.tps)
        part = G.at[s, chunk_rows(i)]
        return remote(part, part, v["gs"].at[side, s, i], v["gr"].at[side, s, i], (rep, to))

    is_end = (tp == 0) | (tp == last)
    is_helper = (tp == 1) | (tp == last - 1)

    def comes(side, d, j):
        s = tp - d if side == 0 else tp + d
        inside = s >= 0 if side == 0 else s <= last
        return s, inside & (~is_end | (j < WHOLE)) if d == 1 else inside

    def goes(side, d, j):
        s = tp - d if side == 0 else tp + d
        if side == 0:
            ok = (s >= 0) & (tp < last)
            return s, ok & ((tp != last - 1) | (j < WHOLE)) if d == 0 else ok & comes(0, d, j)[1]
        ok = (s <= last) & (tp > 0)
        return s, ok & ((tp != 1) | (j < WHOLE)) if d == 0 else ok & comes(1, d, j)[1]

    def send_own(i):
        for side in range(2):

            @pl.when(goes(side, 0, i)[1])
            def _():
                hop(side, tp, i).start()

    share = z.feat // z.reps

    def weight_share(q):
        return WX.at[pl.ds(pl.multiple_of(q * share, share), share)]

    def weight_copy():
        helper = jnp.where(tp == 0, 1, last - 1)
        at = pl.multiple_of(helper * z.feat + rep * share, share)
        return remote(
            v["wq"].at[pl.ds(at, share)], weight_share(rep), v["xs"].at[0], v["xr"].at[rep], (rep, helper)
        )

    def weight_peer(k):
        part = weight_share(rep)
        return remote(part, part, v["xps"].at[k], v["xr"].at[rep], (jnp.bitwise_xor(rep, k), tp))

    def weight_sibling(k):
        q = jnp.bitwise_xor(rep, k)
        part = weight_share(q)
        return remote(part, part, v["xpf"].at[k], v["xr"].at[q], (jnp.bitwise_xor(rep, 1), tp))

    def weight_arrives(q):
        part = weight_share(q)
        remote(part, part, v["xs"].at[0], v["xr"].at[q], (q, tp)).wait_recv()

    def weight_send():
        @pl.when(is_helper)
        def _():
            weight_arrives(rep)
            for k in range(2, z.reps, 2):
                weight_peer(k).start()
            weight_sibling(0).start()

    def weight_forward():
        @pl.when(is_helper)
        def _():
            for k in range(2, z.reps, 2):
                weight_arrives(jnp.bitwise_xor(rep, k))
                weight_sibling(k).start()

    def weight_finish():
        @pl.when(is_helper)
        def _():
            for k in range(1, z.reps, 2):
                weight_arrives(jnp.bitwise_xor(rep, k))

    def partial_copy(i):
        part = PX.at[chunk_rows(i)]
        end = jnp.where(tp == 1, 0, last)
        return remote(part, part, v["pxs"].at[i], v["pxr"].at[i], (rep, end))

    def partial(i):
        rows = chunk_rows(i)
        wide = min(512, z.qcols)
        for n in range(0, z.qcols, wide):
            r = jnp.dot(G[tp, rows, :], WX[:, n : n + wide], preferred_element_type=jnp.float32)
            PX[rows, n : n + wide] = r.astype(jnp.bfloat16)
        partial_copy(i).start()

    def take_partial(i):
        @pl.when(is_end & (i >= WHOLE))
        def _():
            rows = chunk_rows(i)
            partial_copy(i).wait_recv()
            ACC[rows, :] += PX[rows, :].astype(jnp.float32)

    def table_side(side, c):
        column = (c // z.sharing) * HEAD_SIZE + side * z.kv_heads * HEAD_SIZE
        return column // z.portion, column % z.portion

    def table_dst(side):
        return UKV.at[my_tables, :, pl.ds(side * HEAD_SIZE, HEAD_SIZE)]

    for c in range(z.tps):
        for side in range(2):
            owner, column = table_side(side, c)
            src = v["upkv"].at[:, :, pl.ds(column, HEAD_SIZE)]
            if owner == c:

                @pl.when(tp == c)
                def _():
                    pltpu.make_async_copy(src, table_dst(side), v["ukr"].at[side]).start()

            else:

                @pl.when(tp == owner)
                def _():
                    remote(src, table_dst(side), v["uks"].at[side, c], v["ukr"].at[side], (rep, c)).start()

    load_tokens.wait()
    for c in (load_wkv, load_w, load_down, load_upq):
        c.start()
    send_own(0)

    @pl.when(is_end)
    def _():
        weight_copy().start()

    for i in range(1, LEAD):
        send_own(i)

    def group(q):
        return pl.ds(q * z.cap, z.cap)

    def pack(q, dst):
        for j in range(z.cap):
            pick = meta[at_slots + q * z.cap + j]
            dst[q, j * z.seq : (j + 1) * z.seq, :] = T[pick]
            mark = meta[at_marks + q * z.cap + j].astype(jnp.float32)
            MK[q, j : j + 1, :] = jnp.full((1, HEAD_SIZE), mark, jnp.float32)

    def token_copy(q):
        return remote(S.at[q], RX.at[rep], v["as_"].at[q], v["ar"].at[rep], (q, tp))

    def mark_copy(q):
        return remote(MK.at[q], MR.at[rep], v["ms"].at[q], v["mr"].at[rep], (q, tp))

    def return_copy(q):
        return remote(SR.at[group(q)], RB.at[group(rep)], v["ts"].at[q], v["tr"].at[rep], (q, tp))

    load_requests.wait()

    @pl.loop(1, z.reps)
    def _(k):
        q = jnp.bitwise_xor(rep, k)
        pack(q, S)
        token_copy(q).start()
        mark_copy(q).start()

    pack(rep, RX)
    MR[rep] = MK[rep]

    def pair_sums():
        load_wkv.wait()
        half = z.kv_heads * HEAD_SIZE

        @pl.loop(0, z.rows // 128)
        def _(b):
            rows = pl.ds(pl.multiple_of(b * 128, 128), 128)
            x = G[tp, rows, :]
            for side in range(2):
                r = jnp.dot(x, WKV[:, side * half : (side + 1) * half], preferred_element_type=jnp.float32)
                for h in range(z.kv_heads):
                    PO[h, rows, side * HEAD_SIZE : (side + 1) * HEAD_SIZE] = r[
                        :, h * HEAD_SIZE : (h + 1) * HEAD_SIZE
                    ]

    def pair_hop(side, c):
        to = lax.rem(tp + 1, z.tps) if side == 0 else lax.rem(tp + last, z.tps)
        buf = (CR if side == 0 else CL).at[c]
        return remote(buf, buf, v["cs"].at[side, c], v["cr"].at[side, c], (rep, to))

    def pair_step(n):
        for c in reversed(range(z.tps)):
            if c > n:

                @pl.when(tp == n)
                def _():
                    own = PO[c // z.sharing]
                    if n > 0:
                        pair_hop(0, c).wait_recv()
                        own = own + CR[c].astype(jnp.float32)
                    CR[c] = own.astype(jnp.bfloat16)
                    pair_hop(0, c).start()

        for c in range(z.tps):
            if c < last - n:

                @pl.when(tp == last - n)
                def _():
                    own = PO[c // z.sharing]
                    if n > 0:
                        pair_hop(1, c).wait_recv()
                        own = own + CL[c].astype(jnp.float32)
                    CL[c] = own.astype(jnp.bfloat16)
                    pair_hop(1, c).start()

    def pair_finish():
        @pl.when(tp > 0)
        def _():
            pair_hop(0, tp).wait_recv()
            PO[head] = PO[head] + CR[tp].astype(jnp.float32)

        @pl.when(tp < last)
        def _():
            pair_hop(1, tp).wait_recv()
            PO[head] = PO[head] + CL[tp].astype(jnp.float32)

    def shrink_of(q):
        x = RX[q]
        parts = [nt_dot(x, DN[a * z.outs : (a + 1) * z.outs, :]) for a in range(z.tables)]
        for j in range(z.cap):
            mark = MR[q, j : j + 1, 0:1]
            total = jnp.zeros((z.seq, z.outs), jnp.float32)
            for a in range(z.tables):
                total = jnp.where(mark == float(a), parts[a][j * z.seq : (j + 1) * z.seq], total)
            low = jnp.concatenate([total, jnp.zeros((z.seq, LOW - z.outs), jnp.float32)], axis=1)
            SR[q * z.cap + j] = low.astype(jnp.bfloat16)

    def up_copies(q, source, send_q, send_v):
        part = pl.ds(source * z.tables, z.tables)
        return (
            remote(UQ.at[part], UQ.at[part], send_q, v["uqr"].at[source], (q, tp)),
            remote(UKV.at[part], UKV.at[part], send_v, v["ver"].at[source], (q, tp)),
        )

    def peer_copies(k):
        q = jnp.bitwise_xor(rep, k)
        return up_copies(q, rep, v["uqs"].at[k], v["ves"].at[k])

    def sibling_copies(k):
        return up_copies(jnp.bitwise_xor(rep, 1), jnp.bitwise_xor(rep, k), v["uqf"].at[k], v["vef"].at[k])

    def shrink_step(lo, hi):
        if lo == 0:
            load_down.wait()

        @pl.loop(lo, hi)
        def _(k):
            q = jnp.bitwise_xor(rep, k)

            @pl.when(k > 0)
            def _():
                token_copy(q).wait_send()
                mark_copy(q).wait_send()
                remote(S.at[q], RX.at[q], v["as_"].at[q], v["ar"].at[q], (q, tp)).wait_recv()
                remote(MK.at[q], MR.at[q], v["ms"].at[q], v["mr"].at[q], (q, tp)).wait_recv()

            shrink_of(q)

            @pl.when(k > 0)
            def _():
                return_copy(q).start()

            @pl.when(k == 0)
            def _():
                RB[group(rep)] = SR[group(rep)]

    def up_send():
        load_upq.wait()
        for side in range(2):
            pltpu.make_async_copy(table_dst(side), table_dst(side), v["ukr"].at[side]).wait()
        for k in range(2, z.reps, 2):
            for c in peer_copies(k):
                c.start()
        for c in sibling_copies(0):
            c.start()

    def up_forward():
        for k in range(2, z.reps, 2):
            q = jnp.bitwise_xor(rep, k)
            for c in up_copies(q, q, v["uqs"].at[k], v["ves"].at[k]):
                c.wait_recv()
            for c in sibling_copies(k):
                c.start()

    def up_finish():
        for k in range(0, z.reps, 2):
            q = jnp.bitwise_xor(rep, k + 1)
            for c in up_copies(q, q, v["uqf"].at[k], v["vef"].at[k]):
                c.wait_recv()

    def piece(c):
        return pl.ds(pl.multiple_of(c * z.piece, z.piece), z.piece)

    def scatter_copy(c):
        return remote(PH.at[piece(c)], RSB.at[tp], v["rss"].at[c], v["rsr"].at[tp], (rep, c))

    def gather_copy(c):
        return remote(SH.at[piece(tp)], SH.at[piece(tp)], v["ags"].at[c], v["agr"].at[tp], (rep, c))

    def home_step():
        @pl.loop(1, z.reps)
        def _(k):
            q = jnp.bitwise_xor(rep, k)
            remote(SR.at[group(q)], RB.at[group(q)], v["ts"].at[q], v["tr"].at[q], (q, tp)).wait_recv()

        @pl.loop(0, z.requests)
        def _(r):
            PH[pl.ds(pl.multiple_of(r * z.seq, z.seq), z.seq), :] = RB[meta[at_ids + r]]

        for d in range(1, z.tps):
            scatter_copy(other_tp(d)).start()

    def sum_step():
        total = PH[piece(tp), :].astype(jnp.float32)
        for d in range(1, z.tps):
            c = other_tp(d)
            remote(PH.at[piece(c)], RSB.at[c], v["rss"].at[c], v["rsr"].at[c], (rep, c)).wait_recv()
            total = total + RSB[c].astype(jnp.float32)
        SH[piece(tp), :] = total.astype(jnp.bfloat16)
        for d in range(1, z.tps):
            gather_copy(other_tp(d)).start()

    def sum_finish():
        for d in range(1, z.tps):
            c = other_tp(d)
            remote(SH.at[piece(c)], SH.at[piece(c)], v["ags"].at[c], v["agr"].at[c], (rep, c)).wait_recv()

    def project(s, i, first):
        rows = chunk_rows(i)
        x = G[s, rows, :]
        wide = min(512, z.qcols)
        for n in range(0, z.qcols, wide):
            r = jnp.dot(
                x,
                W[pl.ds(pl.multiple_of(s * z.feat, z.feat), z.feat), n : n + wide],
                preferred_element_type=jnp.float32,
            )
            if first:
                ACC[rows, n : n + wide] = r
            else:
                ACC[rows, n : n + wide] += r

    heads = z.qcols // HEAD_SIZE
    cos = v["cosine"][...]
    sin = v["sine"][...]

    def rotate(x):
        return (x * cos + pltpu.roll(x, HALF, 1) * sin).astype(jnp.bfloat16)

    def attend_request(r):
        rows = pl.ds(pl.multiple_of(r * z.seq, z.seq), z.seq)
        table = meta[at_homes + r]
        size = meta[at_sizes + r]
        low = SH[rows, :]

        def change(side, up):
            d = jnp.dot(low[:, side * z.rank : (side + 1) * z.rank], up, preferred_element_type=jnp.float32)
            return (adapter_scale * d).astype(jnp.bfloat16).astype(jnp.float32)

        up_kv = UKV[table]
        base = PO[head, rows, :]
        keys_raw = (base[:, :HEAD_SIZE] + change(1, up_kv[:, :HEAD_SIZE])).astype(jnp.bfloat16)
        values = (base[:, HEAD_SIZE:] + change(2, up_kv[:, HEAD_SIZE:])).astype(jnp.bfloat16)
        keys = rotate(keys_raw.astype(jnp.float32))
        raw = ACC[rows, :] + change(0, UQ[table])
        query = jnp.concatenate(
            [rotate(raw[:, h * HEAD_SIZE : (h + 1) * HEAD_SIZE]) for h in range(heads)], axis=0
        )
        scores = nt_dot(keys, query) * (1.0 / math.sqrt(HEAD_SIZE))
        p_at = lax.broadcasted_iota(jnp.int32, scores.shape, 0)
        q_at = lax.broadcasted_iota(jnp.int32, scores.shape, 1) % z.seq
        scores = jnp.where((p_at <= q_at) & (p_at < size), scores, jnp.float32(-1e30))
        weights = jnp.exp(scores - jnp.max(scores, axis=0, keepdims=True))
        probs = (weights / jnp.sum(weights, axis=0, keepdims=True)).astype(jnp.bfloat16)
        mixed = lax.dot_general(
            probs, values, (((0,), (0,)), ((), ())), preferred_element_type=jnp.float32
        )
        live = lax.broadcasted_iota(jnp.int32, mixed.shape, 0) % z.seq < size
        mixed = jnp.where(live, mixed, 0.0).astype(jnp.bfloat16)
        for h in range(heads):
            OB[rows, h * HEAD_SIZE : (h + 1) * HEAD_SIZE] = mixed[h * z.seq : (h + 1) * z.seq]

    per_chunk = z.chunk // z.seq

    def out_copy(i):
        return pltpu.make_async_copy(OB.at[chunk_rows(i)], out.at[chunk_rows(i)], v["outs"].at[i])

    def attend(lo, hi):
        @pl.loop(lo, hi)
        def _(i):
            take_partial(i)

            @pl.loop(0, per_chunk)
            def _(b):
                attend_request(i * per_chunk + b)

            out_copy(i).start()

    total_hooks = z.hooks

    def scaled(x):
        return x * total_hooks // 30

    first_partial = scaled(18)
    events = {}

    def add(at, what):
        events.setdefault(at, []).append(what)

    add(0, pair_sums)
    for n in range(last):
        add(scaled(3 + 8 * n // (last - 1)), lambda n=n: pair_step(n))
    add(scaled(3), weight_send)
    per_hook = -(-z.reps // 8)
    for j in range(8):
        add(scaled(13) + j, lambda lo=j * per_hook: shrink_step(lo, min(z.reps, lo + per_hook)))
    add(scaled(13), weight_forward)
    add(first_partial, weight_finish)
    add(scaled(17), up_send)
    add(scaled(21), home_step)
    add(scaled(22), sum_step)
    add(scaled(25), pair_finish)
    add(scaled(25), up_forward)
    add(total_hooks - TAIL, up_finish)
    add(total_hooks - TAIL, sum_finish)
    step = -(-(CHUNKS - 1) // (TAIL - 1))
    for j in range(TAIL - 1):
        lo, hi = j * step, min(CHUNKS - 1, j * step + step)
        add(total_hooks - TAIL + j, lambda lo=lo, hi=hi: attend(lo, hi))
    add(total_hooks - 1, lambda: attend(CHUNKS - 1, CHUNKS))

    @pl.loop(0, z.rounds)
    def _(i):
        for d in range(1, z.tps):
            j = i - (d - 1) * SKEW

            @pl.when((j >= 0) & (j < CHUNKS))
            def _():
                for side in range(2):
                    s, ok = comes(side, d, j)

                    @pl.when(ok)
                    def _():
                        hop(side, s, j).wait_recv()

                    @pl.when(goes(side, d, j)[1])
                    def _():
                        hop(side, s, j).start()

                if d == 1:

                    @pl.when(i + LEAD < CHUNKS)
                    def _():
                        send_own(i + LEAD)

                    @pl.when(i == 0)
                    def _():
                        load_w.wait()

                    project(tp, j, True)
                for side in range(2):
                    s, ok = comes(side, d, j)

                    @pl.when(ok)
                    def _():
                        project(s, j, False)

            h = i * last + (d - 1)
            for at in sorted(events):
                if at % last == d - 1:

                    @pl.when(i == at // last)
                    def _():
                        for what in events[at]:
                            what()

            @pl.when((h >= first_partial) & (h < first_partial + CHUNKS - WHOLE) & is_helper)
            def _():
                partial(h - first_partial + WHOLE)

    for side in range(2):
        for d in range(0, last):

            @pl.loop(0, CHUNKS)
            def _(i):
                s, ok = goes(side, d, i)

                @pl.when(ok)
                def _():
                    hop(side, s, i).wait_send()

    @pl.when(is_end)
    def _():
        weight_copy().wait_send()

    @pl.when(is_helper)
    def _():
        for k in range(0, z.reps, 2):
            if k:
                weight_peer(k).wait_send()
            weight_sibling(k).wait_send()
        for i in range(WHOLE, CHUNKS):
            partial_copy(i).wait_send()

    for c in range(z.tps):
        for side in range(2):
            owner, column = table_side(side, c)
            if owner != c:

                @pl.when(tp == owner)
                def _():
                    src = v["upkv"].at[:, :, pl.ds(column, HEAD_SIZE)]
                    remote(src, table_dst(side), v["uks"].at[side, c], v["ukr"].at[side], (rep, c)).wait_send()

        @pl.when(tp < c)
        def _():
            pair_hop(0, c).wait_send()

        @pl.when(tp > c)
        def _():
            pair_hop(1, c).wait_send()

    @pl.loop(1, z.reps)
    def _(k):
        return_copy(jnp.bitwise_xor(rep, k)).wait_send()

    for d in range(1, z.tps):
        scatter_copy(other_tp(d)).wait_send()
        gather_copy(other_tp(d)).wait_send()
    for k in range(0, z.reps, 2):
        if k:
            for c in peer_copies(k):
                c.wait_send()
        for c in sibling_copies(k):
            c.wait_send()
    for i in range(CHUNKS):
        out_copy(i).wait()


def fused(z, meta, tokens, wq, wkv, down, upq, upkv):
    cosine, sine = rope_tables(z.seq)
    by_request = tokens.reshape(z.requests, z.seq, z.feat)
    bf16, f32 = jnp.bfloat16, jnp.float32
    V = pltpu.VMEM
    D = pltpu.SemaphoreType.DMA
    rows_q = z.cap * z.seq
    marks = (z.reps, -(-z.cap // 8) * 8, HEAD_SIZE)
    scratch = [
        V((z.requests, z.seq, z.feat), bf16),
        V((z.tps, z.rows, z.feat), bf16),
        V((z.tps * z.feat, z.qcols), bf16),
        V((z.feat, z.pcols), bf16),
        V((z.tables * z.outs, z.feat), bf16),
        V((z.reps, rows_q, z.feat), bf16),
        V((z.reps, rows_q, z.feat), bf16),
        V(marks, f32),
        V((z.slots, z.seq, LOW), bf16),
        V((z.slots, z.seq, LOW), bf16),
        V((z.rows, LOW), bf16),
        V((z.tps, z.piece, LOW), bf16),
        V((z.rows, LOW), bf16),
        V((z.reps * z.tables, z.rank, z.qcols), bf16),
        V((z.reps * z.tables, z.rank, 2 * HEAD_SIZE), bf16),
        V((z.rows, z.qcols), f32),
        V((z.kv_heads, z.rows, 2 * HEAD_SIZE), f32),
        V((z.tps, z.rows, 2 * HEAD_SIZE), bf16),
        V((z.tps, z.rows, 2 * HEAD_SIZE), bf16),
        V((z.rows, z.qcols), bf16),
        V((z.feat, z.qcols), bf16),
        V((z.rows, z.qcols), bf16),
        V(marks, f32),
        D((6,)),
        D((CHUNKS,)),
        D((2, z.tps, CHUNKS)),
        D((2, z.tps, CHUNKS)),
        D((z.reps,)),
        D((z.reps,)),
        D((z.reps,)),
        D((z.reps,)),
        D((z.reps,)),
        D((z.reps,)),
        D((2, z.tps)),
        D((2, z.tps)),
        D((z.tps,)),
        D((z.tps,)),
        D((z.tps,)),
        D((z.tps,)),
        D((2, z.tps)),
        D((2,)),
        D((z.reps,)),
        D((z.reps,)),
        D((z.reps,)),
        D((z.reps,)),
        D((z.reps,)),
        D((z.reps,)),
        D((1,)),
        D((z.reps,)),
        D((z.reps,)),
        D((z.reps,)),
        D((CHUNKS,)),
        D((CHUNKS,)),
    ]
    vmem = pl.BlockSpec(memory_space=pltpu.VMEM)
    smem = pl.BlockSpec(memory_space=pltpu.SMEM)
    hbm = pl.BlockSpec(memory_space=pl.ANY)
    flops = 2 * z.rows * z.feat * (z.tps * z.qcols + z.pcols)

    def body(*refs):
        fused_kernel(z, *refs)

    return pl.pallas_call(
        body,
        out_shape=jax.ShapeDtypeStruct((z.rows, z.qcols), bf16),
        in_specs=[smem, vmem, vmem] + [hbm] * 7,
        out_specs=hbm,
        scratch_shapes=scratch,
        compiler_params=pltpu.CompilerParams(
            collective_id=0, has_side_effects=True, vmem_limit_bytes=62 << 20
        ),
        cost_estimate=pl.CostEstimate(flops=flops, bytes_accessed=28 << 20, transcendentals=1 << 20),
    )(meta, jnp.asarray(cosine), jnp.asarray(sine), tokens, by_request, wq, wkv, down, upq, upkv)


def shards(
    tokens,
    query_weight,
    key_value_weight,
    adapter_down_tables,
    adapter_up_query,
    adapter_up_key_value,
    request_adapter,
    request_token_length,
    adapter_table_row,
):
    tables, outs, feat = adapter_down_tables.shape
    z = Sizes(
        lax.axis_size("rep"),
        lax.axis_size("tp"),
        tokens.shape,
        query_weight.shape,
        key_value_weight.shape,
        tables,
        adapter_up_query.shape[1],
        request_adapter.shape[0],
        adapter_up_key_value.shape[2],
    )
    match = request_adapter[:, None] == jnp.arange(adapter_table_row.shape[0], dtype=jnp.int32)
    homes = jnp.sum(jnp.where(match, adapter_table_row[None, :], 0), axis=1)
    owners = homes // tables
    pos = jnp.arange(z.requests, dtype=jnp.int32)
    earlier = (owners[:, None] == owners[None, :]) & (pos[None, :] < pos[:, None])
    slot_ids = owners * z.cap + jnp.sum(earlier.astype(jnp.int32), axis=1)
    slot_at = jnp.arange(z.slots, dtype=jnp.int32)
    taken = slot_ids[None, :] == slot_at[:, None]
    picks = jnp.sum(jnp.where(taken, pos, 0), axis=1)
    slot_local = jnp.sum(jnp.where(taken, (homes % tables)[None, :], 0), axis=1)
    meta = jnp.concatenate([picks, slot_local, slot_ids, homes, request_token_length])
    meta = meta.astype(jnp.int32)
    return fused(
        z,
        meta,
        tokens,
        query_weight,
        key_value_weight,
        adapter_down_tables.reshape(tables * outs, feat),
        adapter_up_query,
        adapter_up_key_value,
    )


def solution(mesh):
    placed = (
        P("rep", "tp"),
        P(None, "tp"),
        P("tp", None),
        P("rep", None, "tp"),
        P("rep", None, "tp"),
        P("rep", None, "tp"),
        P("rep"),
        P("rep"),
        P(),
    )
    return jax.shard_map(
        shards, mesh=mesh, in_specs=placed, out_specs=P("rep", "tp"), check_vma=False
    )
```

```python
import math

import jax
import jax.numpy as jnp
import numpy as np
from jax import lax
from jax.experimental import pallas as pl
from jax.experimental.pallas import tpu as pltpu
from jax.sharding import PartitionSpec as P

HEAD_SIZE = 128
HALF = HEAD_SIZE // 2
SIDES = 3
LOW = 256
CHUNKS = 8
LEAD = 2
TAIL = 3
WHOLE = 3
SKEW = 1

adapter_scale = 0.5
rope_theta = 500000.0
MESH = pl.DeviceIdType.MESH


def rope_tables(seq_len):
    frequency = np.float64(rope_theta) ** (-(np.arange(HALF, dtype=np.float64) * 2.0 / HEAD_SIZE))
    angles = np.arange(seq_len).astype(np.float64)[:, None] * frequency[None, :]
    cosine = np.concatenate([np.cos(angles), np.cos(angles)], axis=1)
    sine = np.concatenate([-np.sin(angles), np.sin(angles)], axis=1)
    return cosine.astype(np.float32), sine.astype(np.float32)


def nt_dot(a, b):
    return lax.dot_general(a, b, (((1,), (1,)), ((), ())), preferred_element_type=jnp.float32)


class Sizes:
    def __init__(self, replicas, tps, tokens, wq, wkv, tables, rank, requests, portion):
        self.reps = replicas
        self.tps = tps
        self.rows, self.feat = tokens
        self.qcols = wq[1]
        self.pcols = wkv[1]
        self.tables = tables
        self.rank = rank
        self.outs = SIDES * rank
        self.requests = requests
        self.seq = self.rows // requests
        self.cap = max(1, 2 * requests // replicas)
        self.slots = self.cap * replicas
        self.kv_heads = self.pcols // (2 * HEAD_SIZE)
        self.sharing = tps // self.kv_heads
        self.portion = portion
        self.chunk = self.rows // CHUNKS
        self.piece = self.rows // tps
        self.rounds = CHUNKS + (tps - 2) * SKEW
        self.hooks = self.rounds * (tps - 1)


def fused_kernel(z, *refs):
    names = (
        "meta", "cosine", "sine", "tokens", "by_request", "wq", "wkv", "down", "upq",
        "upkv", "out", "T", "G", "W", "WKV", "DN", "S", "RX", "MR", "SR", "RB", "PH", "RSB", "SH",
        "UQ", "UKV", "ACC", "PO", "CR", "CL", "OB", "WX", "PX", "MK", "loc", "outs", "gs", "gr", "as_", "ar", "ms",
        "mr", "ts", "tr", "cs", "cr", "rss", "rsr", "ags", "agr", "uks", "ukr", "uqs", "uqr",
        "uqf", "ves", "ver", "vef", "xs", "xr", "xps", "xpf", "pxs", "pxr",
    )
    v = dict(zip(names, refs))
    meta, tokens, out = v["meta"], v["tokens"], v["out"]
    G, W, WKV, DN, S, RX, MR, SR, RB = (v[n] for n in names[names.index("G") : names.index("PH")])
    PH, RSB, SH, UQ, UKV, ACC, PO, CR, CL, OB, WX, PX, MK = (
        v[n] for n in names[names.index("PH") : names.index("loc")]
    )
    loc = v["loc"]
    rep = lax.axis_index("rep")
    tp = lax.axis_index("tp")
    last = z.tps - 1
    head = tp // z.sharing
    at_slots, at_marks, at_ids = 0, z.slots, 2 * z.slots
    at_homes, at_sizes = at_ids + z.requests, at_ids + 2 * z.requests

    def remote(src, dst, send, recv, to):
        return pltpu.make_async_remote_copy(
            src_ref=src, dst_ref=dst, send_sem=send, recv_sem=recv, device_id=to, device_id_type=MESH
        )

    def other_tp(d):
        return lax.rem(tp + d, z.tps)

    T = v["T"]
    load_tokens = pltpu.make_async_copy(tokens, G.at[tp], loc.at[0])
    load_requests = pltpu.make_async_copy(v["by_request"], T, loc.at[5])
    load_wkv = pltpu.make_async_copy(v["wkv"], WKV, loc.at[1])
    load_w = pltpu.make_async_copy(v["wq"], W, loc.at[2])
    load_down = pltpu.make_async_copy(v["down"], DN, loc.at[3])
    my_tables = pl.ds(rep * z.tables, z.tables)
    load_upq = pltpu.make_async_copy(v["upq"], UQ.at[my_tables], loc.at[4])
    for c in (load_tokens, load_requests):
        c.start()

    barrier = pltpu.get_barrier_semaphore()
    for k in range(1, z.reps):
        pl.semaphore_signal(barrier, inc=1, device_id=(jnp.bitwise_xor(rep, k), tp), device_id_type=MESH)
    for d in range(1, z.tps):
        pl.semaphore_signal(barrier, inc=1, device_id=(rep, other_tp(d)), device_id_type=MESH)
    pl.semaphore_wait(barrier, z.reps - 1 + z.tps - 1)

    def chunk_rows(i):
        return pl.ds(pl.multiple_of(i * z.chunk, z.chunk), z.chunk)

    def hop(side, s, i):
        to = lax.rem(tp + 1, z.tps) if side == 0 else lax.rem(tp + last, z.tps)
        part = G.at[s, chunk_rows(i)]
        return remote(part, part, v["gs"].at[side, s, i], v["gr"].at[side, s, i], (rep, to))

    is_end = (tp == 0) | (tp == last)
    is_helper = (tp == 1) | (tp == last - 1)

    def comes(side, d, j):
        s = tp - d if side == 0 else tp + d
        inside = s >= 0 if side == 0 else s <= last
        return s, inside & (~is_end | (j < WHOLE)) if d == 1 else inside

    def goes(side, d, j):
        s = tp - d if side == 0 else tp + d
        if side == 0:
            ok = (s >= 0) & (tp < last)
            return s, ok & ((tp != last - 1) | (j < WHOLE)) if d == 0 else ok & comes(0, d, j)[1]
        ok = (s <= last) & (tp > 0)
        return s, ok & ((tp != 1) | (j < WHOLE)) if d == 0 else ok & comes(1, d, j)[1]

    def send_own(i):
        for side in range(2):

            @pl.when(goes(side, 0, i)[1])
            def _():
                hop(side, tp, i).start()

    share = z.feat // z.reps

    def weight_share(q):
        return WX.at[pl.ds(pl.multiple_of(q * share, share), share)]

    def weight_copy():
        helper = jnp.where(tp == 0, 1, last - 1)
        at = pl.multiple_of(helper * z.feat + rep * share, share)
        return remote(
            v["wq"].at[pl.ds(at, share)], weight_share(rep), v["xs"].at[0], v["xr"].at[rep], (rep, helper)
        )

    def weight_peer(k):
        part = weight_share(rep)
        return remote(part, part, v["xps"].at[k], v["xr"].at[rep], (jnp.bitwise_xor(rep, k), tp))

    def weight_sibling(k):
        q = jnp.bitwise_xor(rep, k)
        part = weight_share(q)
        return remote(part, part, v["xpf"].at[k], v["xr"].at[q], (jnp.bitwise_xor(rep, 1), tp))

    def weight_arrives(q):
        part = weight_share(q)
        remote(part, part, v["xs"].at[0], v["xr"].at[q], (q, tp)).wait_recv()

    def weight_send():
        @pl.when(is_helper)
        def _():
            weight_arrives(rep)
            for k in range(2, z.reps, 2):
                weight_peer(k).start()
            weight_sibling(0).start()

    def weight_forward():
        @pl.when(is_helper)
        def _():
            for k in range(2, z.reps, 2):
                weight_arrives(jnp.bitwise_xor(rep, k))
                weight_sibling(k).start()

    def weight_finish():
        @pl.when(is_helper)
        def _():
            for k in range(1, z.reps, 2):
                weight_arrives(jnp.bitwise_xor(rep, k))

    def partial_copy(i):
        part = PX.at[chunk_rows(i)]
        end = jnp.where(tp == 1, 0, last)
        return remote(part, part, v["pxs"].at[i], v["pxr"].at[i], (rep, end))

    def partial(i):
        rows = chunk_rows(i)
        wide = min(512, z.qcols)
        for n in range(0, z.qcols, wide):
            r = jnp.dot(G[tp, rows, :], WX[:, n : n + wide], preferred_element_type=jnp.float32)
            PX[rows, n : n + wide] = r.astype(jnp.bfloat16)
        partial_copy(i).start()

    def take_partial(i):
        @pl.when(is_end & (i >= WHOLE))
        def _():
            rows = chunk_rows(i)
            partial_copy(i).wait_recv()
            ACC[rows, :] += PX[rows, :].astype(jnp.float32)

    def table_side(side, c):
        column = (c // z.sharing) * HEAD_SIZE + side * z.kv_heads * HEAD_SIZE
        return column // z.portion, column % z.portion

    def table_dst(side):
        return UKV.at[my_tables, :, pl.ds(side * HEAD_SIZE, HEAD_SIZE)]

    for c in range(z.tps):
        for side in range(2):
            owner, column = table_side(side, c)
            src = v["upkv"].at[:, :, pl.ds(column, HEAD_SIZE)]
            if owner == c:

                @pl.when(tp == c)
                def _():
                    pltpu.make_async_copy(src, table_dst(side), v["ukr"].at[side]).start()

            else:

                @pl.when(tp == owner)
                def _():
                    remote(src, table_dst(side), v["uks"].at[side, c], v["ukr"].at[side], (rep, c)).start()

    load_tokens.wait()
    for c in (load_wkv, load_w, load_down, load_upq):
        c.start()
    send_own(0)

    @pl.when(is_end)
    def _():
        weight_copy().start()

    for i in range(1, LEAD):
        send_own(i)

    def group(q):
        return pl.ds(q * z.cap, z.cap)

    def pack(q, dst):
        for j in range(z.cap):
            pick = meta[at_slots + q * z.cap + j]
            dst[q, j * z.seq : (j + 1) * z.seq, :] = T[pick]
            mark = meta[at_marks + q * z.cap + j].astype(jnp.float32)
            MK[q, j : j + 1, :] = jnp.full((1, HEAD_SIZE), mark, jnp.float32)

    def token_copy(q):
        return remote(S.at[q], RX.at[rep], v["as_"].at[q], v["ar"].at[rep], (q, tp))

    def mark_copy(q):
        return remote(MK.at[q], MR.at[rep], v["ms"].at[q], v["mr"].at[rep], (q, tp))

    def return_copy(q):
        return remote(SR.at[group(q)], RB.at[group(rep)], v["ts"].at[q], v["tr"].at[rep], (q, tp))

    load_requests.wait()

    @pl.loop(1, z.reps)
    def _(k):
        q = jnp.bitwise_xor(rep, k)
        pack(q, S)
        token_copy(q).start()
        mark_copy(q).start()

    pack(rep, RX)
    MR[rep] = MK[rep]

    def pair_sums():
        load_wkv.wait()
        half = z.kv_heads * HEAD_SIZE

        @pl.loop(0, z.rows // 128)
        def _(b):
            rows = pl.ds(pl.multiple_of(b * 128, 128), 128)
            x = G[tp, rows, :]
            for side in range(2):
                r = jnp.dot(x, WKV[:, side * half : (side + 1) * half], preferred_element_type=jnp.float32)
                for h in range(z.kv_heads):
                    PO[h, rows, side * HEAD_SIZE : (side + 1) * HEAD_SIZE] = r[
                        :, h * HEAD_SIZE : (h + 1) * HEAD_SIZE
                    ]

    def pair_hop(side, c):
        to = lax.rem(tp + 1, z.tps) if side == 0 else lax.rem(tp + last, z.tps)
        buf = (CR if side == 0 else CL).at[c]
        return remote(buf, buf, v["cs"].at[side, c], v["cr"].at[side, c], (rep, to))

    def pair_step(n):
        for c in reversed(range(z.tps)):
            if c > n:

                @pl.when(tp == n)
                def _():
                    own = PO[c // z.sharing]
                    if n > 0:
                        pair_hop(0, c).wait_recv()
                        own = own + CR[c].astype(jnp.float32)
                    CR[c] = own.astype(jnp.bfloat16)
                    pair_hop(0, c).start()

        for c in range(z.tps):
            if c < last - n:

                @pl.when(tp == last - n)
                def _():
                    own = PO[c // z.sharing]
                    if n > 0:
                        pair_hop(1, c).wait_recv()
                        own = own + CL[c].astype(jnp.float32)
                    CL[c] = own.astype(jnp.bfloat16)
                    pair_hop(1, c).start()

    def pair_finish():
        @pl.when(tp > 0)
        def _():
            pair_hop(0, tp).wait_recv()
            PO[head] = PO[head] + CR[tp].astype(jnp.float32)

        @pl.when(tp < last)
        def _():
            pair_hop(1, tp).wait_recv()
            PO[head] = PO[head] + CL[tp].astype(jnp.float32)

    def shrink_of(q):
        x = RX[q]
        parts = [nt_dot(x, DN[a * z.outs : (a + 1) * z.outs, :]) for a in range(z.tables)]
        for j in range(z.cap):
            mark = MR[q, j : j + 1, 0:1]
            total = jnp.zeros((z.seq, z.outs), jnp.float32)
            for a in range(z.tables):
                total = jnp.where(mark == float(a), parts[a][j * z.seq : (j + 1) * z.seq], total)
            low = jnp.concatenate([total, jnp.zeros((z.seq, LOW - z.outs), jnp.float32)], axis=1)
            SR[q * z.cap + j] = low.astype(jnp.bfloat16)

    def up_copies(q, source, send_q, send_v):
        part = pl.ds(source * z.tables, z.tables)
        return (
            remote(UQ.at[part], UQ.at[part], send_q, v["uqr"].at[source], (q, tp)),
            remote(UKV.at[part], UKV.at[part], send_v, v["ver"].at[source], (q, tp)),
        )

    def peer_copies(k):
        q = jnp.bitwise_xor(rep, k)
        return up_copies(q, rep, v["uqs"].at[k], v["ves"].at[k])

    def sibling_copies(k):
        return up_copies(jnp.bitwise_xor(rep, 1), jnp.bitwise_xor(rep, k), v["uqf"].at[k], v["vef"].at[k])

    def shrink_step(lo, hi):
        if lo == 0:
            load_down.wait()

        @pl.loop(lo, hi)
        def _(k):
            q = jnp.bitwise_xor(rep, k)

            @pl.when(k > 0)
            def _():
                token_copy(q).wait_send()
                mark_copy(q).wait_send()
                remote(S.at[q], RX.at[q], v["as_"].at[q], v["ar"].at[q], (q, tp)).wait_recv()
                remote(MK.at[q], MR.at[q], v["ms"].at[q], v["mr"].at[q], (q, tp)).wait_recv()

            shrink_of(q)

            @pl.when(k > 0)
            def _():
                return_copy(q).start()

            @pl.when(k == 0)
            def _():
                RB[group(rep)] = SR[group(rep)]

    def up_send():
        load_upq.wait()
        for side in range(2):
            pltpu.make_async_copy(table_dst(side), table_dst(side), v["ukr"].at[side]).wait()
        for k in range(2, z.reps, 2):
            for c in peer_copies(k):
                c.start()
        for c in sibling_copies(0):
            c.start()

    def up_forward():
        for k in range(2, z.reps, 2):
            q = jnp.bitwise_xor(rep, k)
            for c in up_copies(q, q, v["uqs"].at[k], v["ves"].at[k]):
                c.wait_recv()
            for c in sibling_copies(k):
                c.start()

    def up_finish():
        for k in range(0, z.reps, 2):
            q = jnp.bitwise_xor(rep, k + 1)
            for c in up_copies(q, q, v["uqf"].at[k], v["vef"].at[k]):
                c.wait_recv()

    def piece(c):
        return pl.ds(pl.multiple_of(c * z.piece, z.piece), z.piece)

    def scatter_copy(c):
        return remote(PH.at[piece(c)], RSB.at[tp], v["rss"].at[c], v["rsr"].at[tp], (rep, c))

    def gather_copy(c):
        return remote(SH.at[piece(tp)], SH.at[piece(tp)], v["ags"].at[c], v["agr"].at[tp], (rep, c))

    def home_step():
        @pl.loop(1, z.reps)
        def _(k):
            q = jnp.bitwise_xor(rep, k)
            remote(SR.at[group(q)], RB.at[group(q)], v["ts"].at[q], v["tr"].at[q], (q, tp)).wait_recv()

        @pl.loop(0, z.requests)
        def _(r):
            PH[pl.ds(pl.multiple_of(r * z.seq, z.seq), z.seq), :] = RB[meta[at_ids + r]]

        for d in range(1, z.tps):
            scatter_copy(other_tp(d)).start()

    def sum_step():
        total = PH[piece(tp), :].astype(jnp.float32)
        for d in range(1, z.tps):
            c = other_tp(d)
            remote(PH.at[piece(c)], RSB.at[c], v["rss"].at[c], v["rsr"].at[c], (rep, c)).wait_recv()
            total = total + RSB[c].astype(jnp.float32)
        SH[piece(tp), :] = total.astype(jnp.bfloat16)
        for d in range(1, z.tps):
            gather_copy(other_tp(d)).start()

    def sum_finish():
        for d in range(1, z.tps):
            c = other_tp(d)
            remote(SH.at[piece(c)], SH.at[piece(c)], v["ags"].at[c], v["agr"].at[c], (rep, c)).wait_recv()

    def project(s, i, first):
        rows = chunk_rows(i)
        x = G[s, rows, :]
        wide = min(512, z.qcols)
        for n in range(0, z.qcols, wide):
            r = jnp.dot(
                x,
                W[pl.ds(pl.multiple_of(s * z.feat, z.feat), z.feat), n : n + wide],
                preferred_element_type=jnp.float32,
            )
            if first:
                ACC[rows, n : n + wide] = r
            else:
                ACC[rows, n : n + wide] += r

    heads = z.qcols // HEAD_SIZE
    cos = v["cosine"][...]
    sin = v["sine"][...]

    def rotate(x):
        return (x * cos + pltpu.roll(x, HALF, 1) * sin).astype(jnp.bfloat16)

    def attend_request(r):
        rows = pl.ds(pl.multiple_of(r * z.seq, z.seq), z.seq)
        table = meta[at_homes + r]
        size = meta[at_sizes + r]
        low = SH[rows, :]

        def change(side, up):
            d = jnp.dot(low[:, side * z.rank : (side + 1) * z.rank], up, preferred_element_type=jnp.float32)
            return (adapter_scale * d).astype(jnp.bfloat16).astype(jnp.float32)

        up_kv = UKV[table]
        base = PO[head, rows, :]
        keys_raw = (base[:, :HEAD_SIZE] + change(1, up_kv[:, :HEAD_SIZE])).astype(jnp.bfloat16)
        values = (base[:, HEAD_SIZE:] + change(2, up_kv[:, HEAD_SIZE:])).astype(jnp.bfloat16)
        keys = rotate(keys_raw.astype(jnp.float32))
        raw = ACC[rows, :] + change(0, UQ[table])
        query = jnp.concatenate(
            [rotate(raw[:, h * HEAD_SIZE : (h + 1) * HEAD_SIZE]) for h in range(heads)], axis=0
        )
        scores = nt_dot(keys, query) * (1.0 / math.sqrt(HEAD_SIZE))
        p_at = lax.broadcasted_iota(jnp.int32, scores.shape, 0)
        q_at = lax.broadcasted_iota(jnp.int32, scores.shape, 1) % z.seq
        scores = jnp.where((p_at <= q_at) & (p_at < size), scores, jnp.float32(-1e30))
        weights = jnp.exp(scores - jnp.max(scores, axis=0, keepdims=True))
        probs = (weights / jnp.sum(weights, axis=0, keepdims=True)).astype(jnp.bfloat16)
        mixed = lax.dot_general(
            probs, values, (((0,), (0,)), ((), ())), preferred_element_type=jnp.float32
        )
        live = lax.broadcasted_iota(jnp.int32, mixed.shape, 0) % z.seq < size
        mixed = jnp.where(live, mixed, 0.0).astype(jnp.bfloat16)
        for h in range(heads):
            OB[rows, h * HEAD_SIZE : (h + 1) * HEAD_SIZE] = mixed[h * z.seq : (h + 1) * z.seq]

    per_chunk = z.chunk // z.seq

    def out_copy(i):
        return pltpu.make_async_copy(OB.at[chunk_rows(i)], out.at[chunk_rows(i)], v["outs"].at[i])

    def attend(lo, hi):
        @pl.loop(lo, hi)
        def _(i):
            take_partial(i)

            @pl.loop(0, per_chunk)
            def _(b):
                attend_request(i * per_chunk + b)

            out_copy(i).start()

    total_hooks = z.hooks

    def scaled(x):
        return x * total_hooks // 30

    first_partial = scaled(18)
    events = {}

    def add(at, what):
        events.setdefault(at, []).append(what)

    add(0, pair_sums)
    for n in range(last):
        add(scaled(3 + 8 * n // (last - 1)), lambda n=n: pair_step(n))
    add(scaled(3), weight_send)
    per_hook = -(-z.reps // 8)
    for j in range(8):
        add(scaled(13) + j, lambda lo=j * per_hook: shrink_step(lo, min(z.reps, lo + per_hook)))
    add(scaled(13), weight_forward)
    add(first_partial, weight_finish)
    add(scaled(17), up_send)
    add(scaled(21), home_step)
    add(scaled(22), sum_step)
    add(scaled(25), pair_finish)
    add(scaled(25), up_forward)
    add(total_hooks - TAIL, up_finish)
    add(total_hooks - TAIL, sum_finish)
    step = -(-(CHUNKS - 1) // (TAIL - 1))
    for j in range(TAIL - 1):
        lo, hi = j * step, min(CHUNKS - 1, j * step + step)
        add(total_hooks - TAIL + j, lambda lo=lo, hi=hi: attend(lo, hi))
    add(total_hooks - 1, lambda: attend(CHUNKS - 1, CHUNKS))

    @pl.loop(0, z.rounds)
    def _(i):
        for d in range(1, z.tps):
            j = i - (d - 1) * SKEW

            @pl.when((j >= 0) & (j < CHUNKS))
            def _():
                for side in range(2):
                    s, ok = comes(side, d, j)

                    @pl.when(ok)
                    def _():
                        hop(side, s, j).wait_recv()

                    @pl.when(goes(side, d, j)[1])
                    def _():
                        hop(side, s, j).start()

                if d == 1:

                    @pl.when(i + LEAD < CHUNKS)
                    def _():
                        send_own(i + LEAD)

                    @pl.when(i == 0)
                    def _():
                        load_w.wait()

                    project(tp, j, True)
                for side in range(2):
                    s, ok = comes(side, d, j)

                    @pl.when(ok)
                    def _():
                        project(s, j, False)

            h = i * last + (d - 1)
            for at in sorted(events):
                if at % last == d - 1:

                    @pl.when(i == at // last)
                    def _():
                        for what in events[at]:
                            what()

            @pl.when((h >= first_partial) & (h < first_partial + CHUNKS - WHOLE) & is_helper)
            def _():
                partial(h - first_partial + WHOLE)

    for side in range(2):
        for d in range(0, last):

            @pl.loop(0, CHUNKS)
            def _(i):
                s, ok = goes(side, d, i)

                @pl.when(ok)
                def _():
                    hop(side, s, i).wait_send()

    @pl.when(is_end)
    def _():
        weight_copy().wait_send()

    @pl.when(is_helper)
    def _():
        for k in range(0, z.reps, 2):
            if k:
                weight_peer(k).wait_send()
            weight_sibling(k).wait_send()
        for i in range(WHOLE, CHUNKS):
            partial_copy(i).wait_send()

    for c in range(z.tps):
        for side in range(2):
            owner, column = table_side(side, c)
            if owner != c:

                @pl.when(tp == owner)
                def _():
                    src = v["upkv"].at[:, :, pl.ds(column, HEAD_SIZE)]
                    remote(src, table_dst(side), v["uks"].at[side, c], v["ukr"].at[side], (rep, c)).wait_send()

        @pl.when(tp < c)
        def _():
            pair_hop(0, c).wait_send()

        @pl.when(tp > c)
        def _():
            pair_hop(1, c).wait_send()

    @pl.loop(1, z.reps)
    def _(k):
        return_copy(jnp.bitwise_xor(rep, k)).wait_send()

    for d in range(1, z.tps):
        scatter_copy(other_tp(d)).wait_send()
        gather_copy(other_tp(d)).wait_send()
    for k in range(0, z.reps, 2):
        if k:
            for c in peer_copies(k):
                c.wait_send()
        for c in sibling_copies(k):
            c.wait_send()
    for i in range(CHUNKS):
        out_copy(i).wait()


def fused(z, meta, tokens, wq, wkv, down, upq, upkv):
    cosine, sine = rope_tables(z.seq)
    by_request = tokens.reshape(z.requests, z.seq, z.feat)
    bf16, f32 = jnp.bfloat16, jnp.float32
    V = pltpu.VMEM
    D = pltpu.SemaphoreType.DMA
    rows_q = z.cap * z.seq
    marks = (z.reps, -(-z.cap // 8) * 8, HEAD_SIZE)
    scratch = [
        V((z.requests, z.seq, z.feat), bf16),
        V((z.tps, z.rows, z.feat), bf16),
        V((z.tps * z.feat, z.qcols), bf16),
        V((z.feat, z.pcols), bf16),
        V((z.tables * z.outs, z.feat), bf16),
        V((z.reps, rows_q, z.feat), bf16),
        V((z.reps, rows_q, z.feat), bf16),
        V(marks, f32),
        V((z.slots, z.seq, LOW), bf16),
        V((z.slots, z.seq, LOW), bf16),
        V((z.rows, LOW), bf16),
        V((z.tps, z.piece, LOW), bf16),
        V((z.rows, LOW), bf16),
        V((z.reps * z.tables, z.rank, z.qcols), bf16),
        V((z.reps * z.tables, z.rank, 2 * HEAD_SIZE), bf16),
        V((z.rows, z.qcols), f32),
        V((z.kv_heads, z.rows, 2 * HEAD_SIZE), f32),
        V((z.tps, z.rows, 2 * HEAD_SIZE), bf16),
        V((z.tps, z.rows, 2 * HEAD_SIZE), bf16),
        V((z.rows, z.qcols), bf16),
        V((z.feat, z.qcols), bf16),
        V((z.rows, z.qcols), bf16),
        V(marks, f32),
        D((6,)),
        D((CHUNKS,)),
        D((2, z.tps, CHUNKS)),
        D((2, z.tps, CHUNKS)),
        D((z.reps,)),
        D((z.reps,)),
        D((z.reps,)),
        D((z.reps,)),
        D((z.reps,)),
        D((z.reps,)),
        D((2, z.tps)),
        D((2, z.tps)),
        D((z.tps,)),
        D((z.tps,)),
        D((z.tps,)),
        D((z.tps,)),
        D((2, z.tps)),
        D((2,)),
        D((z.reps,)),
        D((z.reps,)),
        D((z.reps,)),
        D((z.reps,)),
        D((z.reps,)),
        D((z.reps,)),
        D((1,)),
        D((z.reps,)),
        D((z.reps,)),
        D((z.reps,)),
        D((CHUNKS,)),
        D((CHUNKS,)),
    ]
    vmem = pl.BlockSpec(memory_space=pltpu.VMEM)
    smem = pl.BlockSpec(memory_space=pltpu.SMEM)
    hbm = pl.BlockSpec(memory_space=pl.ANY)
    flops = 2 * z.rows * z.feat * (z.tps * z.qcols + z.pcols)

    def body(*refs):
        fused_kernel(z, *refs)

    return pl.pallas_call(
        body,
        out_shape=jax.ShapeDtypeStruct((z.rows, z.qcols), bf16),
        in_specs=[smem, vmem, vmem] + [hbm] * 7,
        out_specs=hbm,
        scratch_shapes=scratch,
        compiler_params=pltpu.CompilerParams(
            collective_id=0, has_side_effects=True, vmem_limit_bytes=62 << 20
        ),
        cost_estimate=pl.CostEstimate(flops=flops, bytes_accessed=28 << 20, transcendentals=1 << 20),
    )(meta, jnp.asarray(cosine), jnp.asarray(sine), tokens, by_request, wq, wkv, down, upq, upkv)


def shards(
    tokens,
    query_weight,
    key_value_weight,
    adapter_down_tables,
    adapter_up_query,
    adapter_up_key_value,
    request_adapter,
    request_token_length,
    adapter_table_row,
):
    tables, outs, feat = adapter_down_tables.shape
    z = Sizes(
        lax.axis_size("rep"),
        lax.axis_size("tp"),
        tokens.shape,
        query_weight.shape,
        key_value_weight.shape,
        tables,
        adapter_up_query.shape[1],
        request_adapter.shape[0],
        adapter_up_key_value.shape[2],
    )
    match = request_adapter[:, None] == jnp.arange(adapter_table_row.shape[0], dtype=jnp.int32)
    homes = jnp.sum(jnp.where(match, adapter_table_row[None, :], 0), axis=1)
    owners = homes // tables
    pos = jnp.arange(z.requests, dtype=jnp.int32)
    earlier = (owners[:, None] == owners[None, :]) & (pos[None, :] < pos[:, None])
    slot_ids = owners * z.cap + jnp.sum(earlier.astype(jnp.int32), axis=1)
    slot_at = jnp.arange(z.slots, dtype=jnp.int32)
    taken = slot_ids[None, :] == slot_at[:, None]
    picks = jnp.sum(jnp.where(taken, pos, 0), axis=1)
    slot_local = jnp.sum(jnp.where(taken, (homes % tables)[None, :], 0), axis=1)
    meta = jnp.concatenate([picks, slot_local, slot_ids, homes, request_token_length])
    meta = meta.astype(jnp.int32)
    return fused(
        z,
        meta,
        tokens,
        query_weight,
        key_value_weight,
        adapter_down_tables.reshape(tables * outs, feat),
        adapter_up_query,
        adapter_up_key_value,
    )


def solution(mesh):
    placed = (
        P("rep", "tp"),
        P(None, "tp"),
        P("tp", None),
        P("rep", None, "tp"),
        P("rep", None, "tp"),
        P("rep", None, "tp"),
        P("rep"),
        P("rep"),
        P(),
    )
    return jax.shard_map(
        shards, mesh=mesh, in_specs=placed, out_specs=P("rep", "tp"), check_vma=False
    )
```
